32 devices in a mesh: section: 2 (over core), dp: 4 (over z), mp: 4 (over y, x).
Axes of the slice: x: 2, y: 2, z: 4, core: 2. Of those that a mesh axis runs over, the one named last changes fastest.
Arguments:
- states: bfloat16 [2, 512, 4096], P('section', 'dp'), may hold values from -6 to 6
- gains: float32 [2, 4096], P('section'), may hold values from 0.25 to 1.75
- proj_a: bfloat16 [2, 4096, 4096], P('section', None, 'mp'), may hold values from -0.03125 to 0.03125
- proj_b: bfloat16 [2, 4096, 4096], P('section', None, 'mp'), may hold values from -0.09375 to 0.09375
- cotangent: bfloat16 [512, 4096], P('dp'), may hold values from -12 to 12
- src_len: int32 [4, 16], replicated, may hold values from 1 to 16, 128 in all within a row
- tgt_len: int32 [4, 16], replicated, may hold values from 1 to 16, 128 in all within a row
- dest: int32 [4, 16], replicated, may hold values from 0 to 63, as said below
Outputs:
- grad_states: bfloat16 [2, 512, 4096], P('section', 'dp')
- grad_a: float32 [2, 4096, 4096], P('section', 'dp', 'mp')
- grad_b: float32 [2, 4096, 4096], P('section', 'dp', 'mp')
The draws below stay inside these ranges and needn't reach their ends.
Inputs may be any that keep to these rules, and one draw needn't show every extreme that they name: `src_len`: each row sums to 128. `tgt_len`: each row sums to 128. `dest`: every value from 0 to 63 appears once; each row holds exactly 4 values in each range d * 16 to (d + 1) * 16 - 1.
All inputs are finite; a program needn't handle non-finite values.
Results may differ from the reference program's by a relative error of at most 0.014.
Values may be sent and summed in bfloat16 or wider, within the bound.
A program may use at most 128 MiB of HBM per device.

```python
import math
import jax
import jax.numpy as jnp
import numpy as np
from jax import lax

D = 4096
HEAD_DIM = 64
TOK_DEV = 128
SEQ_DEV = 16
INNER = 4096
MAXLEN = 16
ROWS = 512
N_DP = 4


def draw_dest(key, part):
    group = SEQ_DEV // N_DP
    send_key, slot_key = jax.random.split(jax.random.fold_in(key, 17))
    send_perm = jax.vmap(lambda one: jax.random.permutation(one, SEQ_DEV))(jax.random.split(send_key, N_DP)).astype(jnp.int32)
    slot_perm = jax.vmap(lambda one: jax.random.permutation(one, SEQ_DEV))(jax.random.split(slot_key, N_DP)).astype(jnp.int32)
    source = jnp.arange(N_DP, dtype=jnp.int32)[:, None]
    place = jnp.arange(SEQ_DEV, dtype=jnp.int32)[None, :]
    target = place // group
    slot = slot_perm[target, source * group + place % group]
    value = (target * SEQ_DEV + slot).astype(jnp.int32)
    sources = jnp.broadcast_to(source, (N_DP, SEQ_DEV))
    return jnp.zeros((N_DP, SEQ_DEV), jnp.int32).at[sources, send_perm].set(value)


def strengthened(drawn, own_key, source, target, blocks, factor):
    def block_of(position):
        return (jnp.arange(drawn.shape[position]) // (drawn.shape[position] // blocks)).reshape((-1,) + (1,) * (drawn.ndim - 1 - position))

    near = jax.random.permutation(own_key, blocks)[block_of(target)]
    second = (block_of(target) + blocks // 2) % blocks
    return jnp.where((block_of(source) == near) | (block_of(source) == second), factor * drawn, drawn)


def shard_levels(key, extent, cuts, least, high):
    loudness, own = 1.0, jax.random.fold_in(key, 6)
    for axis_at, shards_of in cuts:
        draws = jnp.exp(jax.random.uniform(jax.random.fold_in(own, axis_at), (shards_of,), jnp.float32, least / len(cuts), high / len(cuts)))
        loudness = loudness * jnp.repeat(draws, extent[axis_at] // shards_of).reshape([-1 if axis == axis_at else 1 for axis in range(len(extent))])
    return loudness


def split_up(number_of, total, limit, slope):
    weights = [(1 << 20) // math.isqrt(grade ** slope) + 1 for grade in range(2, number_of + 1)]
    spare, given = total - limit - (number_of - 1), [1] * (number_of - 1)
    while spare > 0:
        free = [i for i in range(number_of - 1) if given[i] < limit]
        pool, budget = sum([weights[i] for i in free]), spare
        for i in free:
            more = min(limit - given[i], max(1, budget * weights[i] // pool), spare)
            given[i] = given[i] + more
            spare = spare - more
    return np.array([limit] + given)


def uneven_parts(key, count, total, reach, lean):
    if count == 2:
        one = jax.random.randint(key, (), max(1, total - reach), min(reach, total - 1) + 1)
        return jnp.stack([one, total - one])
    sizes = jnp.asarray(split_up(count, total, reach, lean), jnp.int32)
    pairs = (count - 1) // 2
    donor, taker = sizes[1:1 + 2 * pairs:2], sizes[2:2 + 2 * pairs:2]
    room = jnp.minimum(donor - 1, reach - taker)
    passed = jax.random.randint(jax.random.fold_in(key, 1), (pairs,), 0, 1 << 20) % (room + 1)
    sizes = sizes.at[1:1 + 2 * pairs:2].set(donor - passed).at[2:2 + 2 * pairs:2].set(taker + passed)
    return sizes[jax.random.permutation(jax.random.fold_in(key, 2), count)]


def gaussian(stream_key, extent, spread, reach, shards=(), held_as=jnp.bfloat16):
    array = jax.random.normal(stream_key, extent, jnp.float32) * spread
    if len(shards) > 0:
        array = shard_levels(stream_key, extent, shards, -0.22, 0.18) * array
    return jnp.clip(array, min=-reach, max=reach).astype(held_as)


def heavy_noise(key, shape, deviation, limit, shards, heavy, kind=jnp.bfloat16):
    drawn = deviation * jax.random.normal(key, shape, jnp.float32)
    if shards:
        drawn = drawn * shard_levels(key, shape, shards, -0.22, 0.18)
    return jnp.clip(strengthened(drawn, jax.random.fold_in(key, 3), *heavy), -limit, limit).astype(kind)


def setup_inputs(seed: int = 0) -> dict:
    key_of = jax.random.split(jax.random.key(seed), 9)
    states = heavy_noise(key_of[0], (2, ROWS, D), 1.0, 6.0, ((0, 2), (1, 4)), (1, 2, 4, 2.0))
    gains = jnp.clip(1.0 + 0.15 * jax.random.normal(key_of[1], (2, D), jnp.float32), 0.25, 1.75)
    proj_a = gaussian(key_of[2], (2, D, INNER), (8 * D) ** -0.5, 0.03125, ((0, 2), (2, 4)))
    proj_b = gaussian(key_of[3], (2, D, INNER), D ** -0.5, 0.09375, ((0, 2), (2, 4)))
    cotangent = gaussian(key_of[4], (ROWS, D), 2.0, 12.0, ((0, 4),))
    src_len = jax.vmap(lambda own: uneven_parts(own, SEQ_DEV, TOK_DEV, MAXLEN, 2))(jax.random.split(key_of[5], N_DP)).reshape((N_DP, SEQ_DEV)).astype(jnp.int32)
    tgt_len = jax.vmap(lambda own: uneven_parts(own, SEQ_DEV, TOK_DEV, MAXLEN, 2))(jax.random.split(key_of[6], N_DP)).reshape((N_DP, SEQ_DEV)).astype(jnp.int32)
    dest = draw_dest(jax.random.fold_in(key_of[8], 71), 0)
    return {"states": states, "gains": gains, "proj_a": proj_a, "proj_b": proj_b, "cotangent": cotangent, "src_len": src_len, "tgt_len": tgt_len, "dest": dest}


EPS = 1e-06

def rms_forward(states_row, gain):
    xf = states_row.astype(jnp.float32)
    scale = lax.rsqrt(lax.optimization_barrier(jnp.mean(xf * xf, axis=-1, keepdims=True)) + EPS)
    return (xf, scale, (xf * scale * gain).astype(jnp.bfloat16))

def rms_backward(xf, scale, gain, dnorm):
    upper = gain * dnorm
    inner = lax.optimization_barrier(jnp.mean(xf * upper, axis=-1, keepdims=True))
    return (scale * upper - xf * scale * scale * scale * inner).astype(jnp.bfloat16)

def starts_of(lengths):
    count = lengths.shape[0]
    local = (jnp.cumsum(lengths, axis=1) - lengths).astype(jnp.int32)
    base = (jnp.arange(count, dtype=jnp.int32) * TOK_DEV)[:, None]
    return ((base + local).reshape(-1).astype(jnp.int32), lengths.reshape(-1).astype(jnp.int32))

def pack(rows, starts, lengths):
    steps = jnp.arange(MAXLEN, dtype=jnp.int32)
    index = starts[:, None] + steps[None, :]
    valid = steps[None, :] < lengths[:, None]
    picked = rows[jnp.minimum(index, rows.shape[0] - 1)]
    return jnp.where(valid[:, :, None], picked, jnp.zeros((), rows.dtype))

def unpack(padded, lengths):
    count, per = lengths.shape
    local = (jnp.cumsum(lengths, axis=1) - lengths).astype(jnp.int32)
    ends = local + lengths
    place = jnp.arange(TOK_DEV, dtype=jnp.int32)
    which = lax.optimization_barrier(jnp.sum((place[None, :, None] >= ends[:, None, :]).astype(jnp.int32), axis=-1)).astype(jnp.int32)
    offset = jnp.take_along_axis(local, which, axis=1)
    device = jnp.arange(count, dtype=jnp.int32)[:, None]
    flat = ((device * per + which) * MAXLEN + place[None, :] - offset).reshape(-1)
    return padded.reshape(-1, padded.shape[-1])[flat]

def attend(own, remote, key_len):
    seqs, length, width = own.shape
    cols = width // 2
    heads = cols // HEAD_DIM
    query = own[..., :cols].reshape(seqs, length, heads, HEAD_DIM)
    dout = own[..., cols:].reshape(seqs, length, heads, HEAD_DIM)
    keys = remote[..., :cols].reshape(seqs, length, heads, HEAD_DIM)
    values = remote[..., cols:].reshape(seqs, length, heads, HEAD_DIM)
    qf, df = (query.astype(jnp.float32), dout.astype(jnp.float32))
    kf, vf = (keys.astype(jnp.float32), values.astype(jnp.float32))
    scores = jnp.einsum('sqhd,skhd->shqk', qf, kf)
    live = jnp.arange(length, dtype=jnp.int32)[None, None, None, :] < key_len[:, None, None, None]
    expo = jnp.where(live, jnp.exp(scores), jnp.float32(0.0))
    weight = expo / lax.optimization_barrier(jnp.sum(expo, axis=-1, keepdims=True))
    weight_b = weight.astype(jnp.bfloat16)
    wbf = weight_b.astype(jnp.float32)
    attended = jnp.einsum('shqk,skhd->sqhd', wbf, vf).astype(jnp.bfloat16)
    dweight = jnp.einsum('sqhd,skhd->shqk', df, vf)
    total = lax.optimization_barrier(jnp.sum(weight * dweight, axis=-1, keepdims=True))
    dscore = (weight * (dweight - total)).astype(jnp.bfloat16).astype(jnp.float32)
    dquery = jnp.einsum('shqk,skhd->sqhd', dscore, kf).astype(jnp.bfloat16)
    dkeys = jnp.einsum('shqk,sqhd->skhd', dscore, qf).astype(jnp.bfloat16)
    dvalues = jnp.einsum('shqk,sqhd->skhd', wbf, df).astype(jnp.bfloat16)
    front = jnp.concatenate([dquery.reshape(seqs, length, cols), attended.reshape(seqs, length, cols)], axis=-1)
    back = jnp.concatenate([dkeys.reshape(seqs, length, cols), dvalues.reshape(seqs, length, cols)], axis=-1)
    return (front, back)

def left_product(left, right):
    return lax.dot_general(left, right, (((0,), (0,)), ((), ())), preferred_element_type=jnp.float32)

def right_product(rows, weight):
    return lax.dot_general(rows, weight, (((1,), (1,)), ((), ())), preferred_element_type=jnp.float32)

def reference(states, gains, proj_a, proj_b, cotangent, src_len, tgt_len, dest):
    enc_x, enc_scale, enc_norm = rms_forward(states[0], gains[0])
    dec_x, dec_scale, dec_norm = rms_forward(states[1], gains[1])
    keys = jnp.dot(enc_norm, proj_a[0], preferred_element_type=jnp.float32).astype(jnp.bfloat16)
    values = jnp.dot(enc_norm, proj_b[0], preferred_element_type=jnp.float32).astype(jnp.bfloat16)
    query = jnp.dot(dec_norm, proj_a[1], preferred_element_type=jnp.float32).astype(jnp.bfloat16)
    dout = jnp.dot(cotangent, proj_b[1], preferred_element_type=jnp.float32).astype(jnp.bfloat16)
    flat_dest = dest.reshape(-1).astype(jnp.int32)
    total = flat_dest.shape[0]
    inverse = jnp.zeros((total,), jnp.int32).at[flat_dest].set(jnp.arange(total, dtype=jnp.int32))
    src_start, src_flat = starts_of(src_len)
    tgt_start, tgt_flat = starts_of(tgt_len)
    remote = pack(jnp.concatenate([keys, values], axis=1), src_start[inverse], src_flat[inverse])
    own = pack(jnp.concatenate([query, dout], axis=1), tgt_start, tgt_flat)
    front, back = attend(own, remote, src_flat[inverse])
    dec_rows = unpack(front, tgt_len)
    enc_rows = unpack(back[flat_dest], src_len)
    cols = proj_a.shape[2]
    dquery, attended = (dec_rows[:, :cols], dec_rows[:, cols:])
    dkeys, dvalues = (enc_rows[:, :cols], enc_rows[:, cols:])
    enc_dnorm = right_product(dkeys, proj_a[0]) + right_product(dvalues, proj_b[0])
    dec_dnorm = right_product(dquery, proj_a[1])
    grad_states = jnp.stack([rms_backward(enc_x, enc_scale, gains[0], enc_dnorm), rms_backward(dec_x, dec_scale, gains[1], dec_dnorm)])
    grad_a = jnp.stack([left_product(enc_norm, dkeys), left_product(dec_norm, dquery)])
    grad_b = jnp.stack([left_product(enc_norm, dvalues), left_product(cotangent, attended)])
    return (grad_states, grad_a, grad_b)
```

```python
import functools

import jax
import jax.numpy as jnp
from jax import lax
from jax.experimental import pallas as pl
from jax.experimental.pallas import tpu as pltpu
from jax.sharding import PartitionSpec as P

HEAD_DIM = 64
LANES = 128
EPS = 1e-06
MESH = pl.DeviceIdType.MESH


def rms_forward(states_row, gain):
    xf = states_row.astype(jnp.float32)
    scale = lax.rsqrt(jnp.mean(xf * xf, axis=-1, keepdims=True) + EPS)
    return (xf, scale, (xf * scale * gain).astype(jnp.bfloat16))


def left_product(left, right):
    return lax.dot_general(
        left, right, (((0,), (0,)), ((), ())), preferred_element_type=jnp.float32
    )


def right_product(rows, weight):
    return lax.dot_general(
        rows, weight, (((1,), (1,)), ((), ())), preferred_element_type=jnp.float32
    )


def sequence_of(lengths, names, tokens):
    slot = jnp.arange(lengths.shape[1], dtype=jnp.int32)
    before = slot[:, None] < slot[None, :]
    starts = jnp.sum(jnp.where(before[None], lengths[:, :, None], 0), axis=1)
    place = jnp.arange(tokens, dtype=jnp.int32)[None, :, None]
    offset = place - starts[:, None, :]
    inside = (offset >= 0) & (offset < lengths[:, None, :])
    return jnp.sum(jnp.where(inside, names[:, None, :], 0), axis=-1).reshape(-1)


def attend_piece(encoder, p, group, id_col, id_row, own, other, out_a, out_b, acc_a, acc_b):
    n, tokens, width = own.shape[1:]
    half = width // 2
    rows = n * tokens
    blocks = n // group
    lane = lax.broadcasted_iota(jnp.int32, (1, LANES), 1) // HEAD_DIM
    zero = jnp.zeros((), jnp.bfloat16)
    f32 = jnp.float32

    def cut(ref, which, c, at):
        lo = pl.multiple_of(which * half + c * LANES, LANES)
        return ref[p, at, :, pl.ds(lo, LANES)].reshape(-1, LANES)

    every = pl.ds(0, n)

    @pl.loop(0, half // LANES)
    def _(c):
        out_cols = pl.ds(pl.multiple_of(p * half + c * LANES, LANES), LANES)

        @pl.when(encoder)
        def _():
            keys, values = cut(own, 0, c, every), cut(own, 1, c, every)
            if blocks > 1:
                acc_a[...] = jnp.zeros_like(acc_a)
                acc_b[...] = jnp.zeros_like(acc_b)

            def block(b):
                at = pl.ds(b * group, group)
                query, dout = cut(other, 0, c, at), cut(other, 1, c, at)
                mask = id_col[...].reshape(rows, 1) == id_row[b]
                dk, dv = None, None
                for h in range(LANES // HEAD_DIM):
                    qh = jnp.where(lane == h, query, zero)
                    dh = jnp.where(lane == h, dout, zero)
                    expo = jnp.exp(jnp.where(mask, right_product(keys, qh), -jnp.inf))
                    weight = expo * (1.0 / jnp.sum(expo, axis=0, keepdims=True))
                    dweight = right_product(values, dh)
                    total = jnp.sum(weight * dweight, axis=0, keepdims=True)
                    dscore = (weight * (dweight - total)).astype(jnp.bfloat16)
                    pk = jnp.dot(dscore, qh, preferred_element_type=f32)
                    pv = jnp.dot(weight.astype(jnp.bfloat16), dh, preferred_element_type=f32)
                    dk = pk if dk is None else dk + pk
                    dv = pv if dv is None else dv + pv
                if blocks == 1:
                    out_a[:, :, out_cols] = dk.astype(jnp.bfloat16).reshape(n, tokens, LANES)
                    out_b[:, :, out_cols] = dv.astype(jnp.bfloat16).reshape(n, tokens, LANES)
                else:
                    acc_a[...] += dk
                    acc_b[...] += dv

            if blocks == 1:
                block(0)
            else:
                pl.loop(0, blocks)(block)
                out_a[:, :, out_cols] = acc_a[...].astype(jnp.bfloat16).reshape(n, tokens, LANES)
                out_b[:, :, out_cols] = acc_b[...].astype(jnp.bfloat16).reshape(n, tokens, LANES)

        @pl.when(jnp.logical_not(encoder))
        def _():
            keys, values = cut(other, 0, c, every), cut(other, 1, c, every)

            def block(b):
                at = pl.ds(b * group, group)
                query, dout = cut(own, 0, c, at), cut(own, 1, c, at)
                ids = id_col[at, :, :].reshape(group * tokens, 1)
                mask = None
                dq, att = None, None
                for h in range(LANES // HEAD_DIM):
                    kh = jnp.where(lane == h, keys, zero)
                    vh = jnp.where(lane == h, values, zero)
                    score = right_product(query, kh)
                    if mask is None:
                        span = group * tokens
                        mask = jnp.concatenate(
                            [ids == id_row[i] for i in range(rows // span)], axis=1
                        )
                    expo = jnp.exp(jnp.where(mask, score, -jnp.inf))
                    weight = expo * (1.0 / jnp.sum(expo, axis=1, keepdims=True))
                    dweight = right_product(dout, vh)
                    total = jnp.sum(weight * dweight, axis=1, keepdims=True)
                    dscore = (weight * (dweight - total)).astype(jnp.bfloat16)
                    pq = jnp.dot(dscore, kh, preferred_element_type=f32)
                    pa = jnp.dot(weight.astype(jnp.bfloat16), vh, preferred_element_type=f32)
                    dq = pq if dq is None else dq + pq
                    att = pa if att is None else att + pa
                shape = (group, tokens, LANES)
                out_a[at, :, out_cols] = dq.astype(jnp.bfloat16).reshape(shape)
                out_b[at, :, out_cols] = att.astype(jnp.bfloat16).reshape(shape)

            if blocks == 1:
                block(0)
            else:
                pl.loop(0, blocks)(block)


def forward_kernel(
    n, m, group, normed, second, id_col, id_row, proj_a, proj_b,
    out_a, out_b, mine_a, mine_b,
    wbuf, paired, own, other, acc_a, acc_b, wsem,
    line_send, line_recv, sec_send, sec_recv, za_send, za_recv, mp_send, mp_recv, loc_sem,
):
    me = lax.axis_index("dp")
    col = lax.axis_index("mp")
    sec = lax.axis_index("section")
    tokens, width = normed.shape
    pieces = wbuf.shape[1]
    half = wbuf.shape[3]
    part = tokens // m
    cols = width // n

    def weight_copy(which, p):
        src = (proj_a, proj_b)[which]
        return pltpu.make_async_copy(
            src.at[0, :, pl.ds(p * half, half)], wbuf.at[which, p], wsem.at[which, p]
        )

    for p in range(pieces):
        for which in (0, 1):
            weight_copy(which, p).start()

    barrier = pltpu.get_barrier_semaphore()
    for j in range(1, n):
        pl.semaphore_signal(
            barrier, inc=1, device_id={"dp": lax.rem(me + j, n)}, device_id_type=MESH
        )
    for j in range(1, m):
        pl.semaphore_signal(
            barrier, inc=1, device_id={"mp": lax.rem(col + j, m)}, device_id_type=MESH
        )
    pl.semaphore_signal(barrier, inc=1, device_id={"section": 1 - sec}, device_id_type=MESH)
    pl.semaphore_wait(barrier, n + m - 1)

    band = pl.ds(pl.multiple_of(col * part, part), part)

    def line_copy(way, s, p):
        chunk = me - s if way == 0 else me + s
        target = me + 1 if way == 0 else me - 1
        src = paired.at[p] if s == 0 else own.at[p, chunk]
        return pltpu.make_async_remote_copy(
            src_ref=src, dst_ref=own.at[p, chunk],
            send_sem=line_send.at[way, s, p], recv_sem=line_recv.at[way, s, p],
            device_id={"dp": target}, device_id_type=MESH,
        )

    def line_ok(way, s):
        if way == 0:
            return jnp.logical_and(me - s >= 0, me < n - 1)
        return jnp.logical_and(me + s <= n - 1, me > 0)

    def got(way, s):
        return me - 1 - s >= 0 if way == 0 else me + 1 + s <= n - 1

    def sec_copy(chunk, p, src):
        return pltpu.make_async_remote_copy(
            src_ref=src, dst_ref=other.at[p, chunk],
            send_sem=sec_send.at[chunk, p], recv_sem=sec_recv.at[chunk, p],
            device_id={"section": 1 - sec}, device_id_type=MESH,
        )

    def za_copy(which, j):
        src, dst = ((normed, mine_a), (second, mine_b))[which]
        peer = lax.rem(me + j, n)
        return pltpu.make_async_remote_copy(
            src_ref=src.at[band, pl.ds(pl.multiple_of(peer * cols, cols), cols)],
            dst_ref=dst.at[me, band, :],
            send_sem=za_send.at[which, j], recv_sem=za_recv.at[which, j],
            device_id={"dp": peer}, device_id_type=MESH,
        )

    def mp_copy(which, j):
        dst = (mine_a, mine_b)[which]
        return pltpu.make_async_remote_copy(
            src_ref=dst.at[:, band, :], dst_ref=dst.at[:, band, :],
            send_sem=mp_send.at[which, j], recv_sem=mp_recv.at[which, j],
            device_id={"mp": lax.rem(col + j, m)}, device_id_type=MESH,
        )

    def local(which):
        src, dst = ((normed, mine_a), (second, mine_b))[which]
        return pltpu.make_async_copy(
            src.at[band, pl.ds(pl.multiple_of(me * cols, cols), cols)],
            dst.at[me, band, :], loc_sem.at[which],
        )

    def keep(p):
        return pltpu.make_async_copy(paired.at[p], own.at[p, me], loc_sem.at[2 + p])

    def second_too(fn):
        fn(0)
        pl.when(sec == 1)(lambda: fn(1))

    for j in range(1, n):
        second_too(lambda which: za_copy(which, j).start())
    second_too(lambda which: local(which).start())

    for p in range(pieces):
        for which in (0, 1):
            weight_copy(which, p).wait()
            rows_in = (normed, second)[which]
            paired[p, :, which * half : (which + 1) * half] = jnp.dot(
                rows_in[...], wbuf[which, p], preferred_element_type=jnp.float32
            ).astype(jnp.bfloat16)
        for way in (0, 1):
            pl.when(line_ok(way, 0))(lambda way=way, p=p: line_copy(way, 0, p).start())
        sec_copy(me, p, paired.at[p]).start()
        keep(p).start()

    def spread(which):
        local(which).wait()
        for j in range(1, n):
            za_copy(which, j).wait_recv()
        for j in range(1, m):
            mp_copy(which, j).start()

    second_too(spread)

    for wave in range(pieces + n - 2):
        for s in range(max(0, wave - pieces + 1), min(n - 1, wave + 1)):
            p = wave - s
            for way in (0, 1):

                @pl.when(got(way, s))
                def _():
                    line_copy(way, s, p).wait_recv()
                    chunk = me - 1 - s if way == 0 else me + 1 + s
                    if s + 1 < n - 1:
                        pl.when(line_ok(way, s + 1))(
                            lambda: line_copy(way, s + 1, p).start()
                        )
                    sec_copy(chunk, p, own.at[p, chunk]).start()

        p = wave - (n - 2)
        if p >= 0:
            keep(p).wait()
            for c in range(n):
                sec_copy(c, p, own.at[p, c]).wait_recv()
            attend_piece(
                sec == 0, p, group, id_col, id_row, own, other, out_a, out_b, acc_a, acc_b
            )

    def finish(which):
        for j in range(1, n):
            za_copy(which, j).wait_send()
        for j in range(1, m):
            mp_copy(which, j).wait()

    second_too(finish)
    for p in range(pieces):
        for s in range(n - 1):
            for way in (0, 1):
                pl.when(line_ok(way, s))(
                    lambda way=way, s=s, p=p: line_copy(way, s, p).wait_send()
                )
        for c in range(n):
            sec_copy(c, p, own.at[p, c]).wait_send()


def forward(n, m, normed, second, id_c, id_r, proj_a, proj_b):
    tokens, width = normed.shape
    inner = proj_a.shape[2]
    half = 2 * LANES
    pieces = inner // half
    rows = n * tokens
    group = max(1, min(n, 512 * 512 // (rows * tokens)))
    blocks = n // group
    grad = jax.ShapeDtypeStruct((n, tokens, inner), jnp.bfloat16)
    mine = jax.ShapeDtypeStruct((n, tokens, width // n), jnp.bfloat16)
    acc = (rows, LANES) if blocks > 1 else (8, LANES)
    dma = pltpu.SemaphoreType.DMA
    vmem = pl.BlockSpec(memory_space=pltpu.VMEM)
    anyw = pl.BlockSpec(memory_space=pltpu.HBM)
    bf16 = jnp.bfloat16
    return pl.pallas_call(
        functools.partial(forward_kernel, n, m, group),
        out_shape=(grad, grad, mine, mine),
        in_specs=[vmem] * 4 + [anyw] * 2,
        out_specs=[vmem, vmem, anyw, anyw],
        scratch_shapes=[
            pltpu.VMEM((2, pieces, width, half), bf16),
            pltpu.VMEM((pieces, tokens, 2 * half), bf16),
            pltpu.VMEM((pieces, n, tokens, 2 * half), bf16),
            pltpu.VMEM((pieces, n, tokens, 2 * half), bf16),
            pltpu.VMEM(acc, jnp.float32), pltpu.VMEM(acc, jnp.float32),
            dma((2, pieces)),
            dma((2, n, pieces)), dma((2, n, pieces)), dma((n, pieces)), dma((n, pieces)),
            dma((2, n)), dma((2, n)), dma((2, m)), dma((2, m)), dma((2 + pieces,)),
        ],
        compiler_params=pltpu.CompilerParams(
            collective_id=0, has_side_effects=True, vmem_limit_bytes=67000000
        ),
        name="forward",
    )(normed, second, id_c.reshape(n, tokens, 1), id_r.reshape(blocks, 1, rows // blocks),
      proj_a, proj_b)


def reduce_kernel(
    m, grad_a, grad_b, proj_a, proj_b, x_ref, gain_ref, result,
    left, wbuf, total, mine, partial, landed, gsem, wsem, send, recv,
):
    me = lax.axis_index("dp")
    col = lax.axis_index("mp")
    encoder = lax.axis_index("section") == 0
    tokens = x_ref.shape[0]
    part = tokens // m
    chunks, step = wbuf.shape[1:3]

    def left_copy(which):
        return pltpu.make_async_copy(
            (grad_a, grad_b)[which].at[me], left.at[which], gsem.at[which]
        )

    def weight_copy(which, c):
        return pltpu.make_async_copy(
            (proj_a, proj_b)[which].at[0, pl.ds(c * step, step), :],
            wbuf.at[which, c], wsem.at[which, c],
        )

    left_copy(0).start()
    pl.when(encoder)(lambda: left_copy(1).start())
    for c in range(chunks):
        weight_copy(0, c).start()
        pl.when(encoder)(lambda c=c: weight_copy(1, c).start())

    barrier = pltpu.get_barrier_semaphore()
    for j in range(1, m):
        pl.semaphore_signal(
            barrier, inc=1, device_id={"mp": lax.rem(col + j, m)}, device_id_type=MESH
        )
    pl.semaphore_wait(barrier, m - 1)

    def scatter(j, c):
        peer = lax.rem(col + j, m)
        rows = pl.ds(pl.multiple_of(peer * part, part), part)
        at = pl.ds(c * step, step)
        return pltpu.make_async_remote_copy(
            src_ref=partial.at[rows, at], dst_ref=landed.at[j, :, at],
            send_sem=send.at[j, c], recv_sem=recv.at[j, c],
            device_id={"mp": peer}, device_id_type=MESH,
        )

    band = pl.ds(pl.multiple_of(col * part, part), part)
    left_copy(0).wait()
    pl.when(encoder)(lambda: left_copy(1).wait())
    for c in range(chunks):
        weight_copy(0, c).wait()
        total[...] = right_product(left[0], wbuf[0, c])

        @pl.when(encoder)
        def _():
            weight_copy(1, c).wait()
            total[...] += right_product(left[1], wbuf[1, c])

        partial[:, c * step : (c + 1) * step] = total[...].astype(jnp.bfloat16)
        mine[:, c * step : (c + 1) * step] = total[band, :]
        for j in range(1, m):
            scatter(j, c).start()
    x = x_ref[band, :].astype(jnp.float32)
    scale = lax.rsqrt(jnp.mean(x * x, axis=-1, keepdims=True) + EPS)
    for j in range(1, m):
        for c in range(chunks):
            scatter(j, c).wait_recv()
    dnorm = mine[...]
    for j in range(1, m):
        dnorm = dnorm + landed[j].astype(jnp.float32)
    upper = gain_ref[...] * dnorm
    inner = jnp.mean(x * upper, axis=-1, keepdims=True)
    result[...] = (scale * upper - x * scale * scale * scale * inner).astype(jnp.bfloat16)
    for j in range(1, m):
        for c in range(chunks):
            scatter(j, c).wait_send()


def reduce_norm(m, grad_a, grad_b, proj_a, proj_b, states, gain):
    tokens, width = states.shape
    inner = proj_a.shape[2]
    part = tokens // m
    step = 4 * LANES
    chunks = width // step
    dma = pltpu.SemaphoreType.DMA
    bf16, f32 = jnp.bfloat16, jnp.float32
    vmem = pl.BlockSpec(memory_space=pltpu.VMEM)
    return pl.pallas_call(
        functools.partial(reduce_kernel, m),
        out_shape=jax.ShapeDtypeStruct((part, width), bf16),
        in_specs=[pl.BlockSpec(memory_space=pltpu.HBM)] * 4 + [vmem] * 2,
        out_specs=vmem,
        scratch_shapes=[
            pltpu.VMEM((2, tokens, inner), bf16),
            pltpu.VMEM((2, chunks, step, inner), bf16),
            pltpu.VMEM((tokens, step), f32),
            pltpu.VMEM((part, width), f32),
            pltpu.VMEM((tokens, width), bf16),
            pltpu.VMEM((m, part, width), bf16),
            dma((2,)), dma((2, chunks)), dma((m, chunks)), dma((m, chunks)),
        ],
        compiler_params=pltpu.CompilerParams(
            collective_id=1, has_side_effects=True, vmem_limit_bytes=66500000
        ),
        name="reduce_norm",
    )(grad_a, grad_b, proj_a, proj_b, states, gain)


def stepwise(states, gains, proj_a, proj_b, cotangent, src_len, tgt_len, dest):
    encoder = lax.axis_index("section") == 0
    member = lax.axis_index("dp")
    n = lax.axis_size("dp")
    m = lax.axis_size("mp")
    gain = gains[0]
    weight_a = proj_a[0]
    weight_b = proj_b[0]
    tokens = states.shape[1]
    _, _, normed = rms_forward(states[0], gain)
    second_left = jnp.where(encoder, normed, cotangent)
    rows = n * tokens
    seqs = tgt_len.shape[1]
    names = jnp.arange(n * seqs, dtype=jnp.int32).reshape(n, seqs)
    id_c = sequence_of(
        jnp.where(encoder, src_len, tgt_len), jnp.where(encoder, dest, names), tokens
    )
    id_r = sequence_of(
        jnp.where(encoder, tgt_len, src_len), jnp.where(encoder, names, dest), tokens
    )
    grad_first, grad_second, mine_a, mine_b = forward(
        n, m, normed, second_left, id_c, id_r, proj_a, proj_b
    )
    mine = reduce_norm(m, grad_first, grad_second, proj_a, proj_b, states[0], gains)
    col = lax.axis_index("mp")
    landed = [mine] + [
        lax.ppermute(mine, "mp", [(i, (i + j) % m) for i in range(m)]) for j in range(1, m)
    ]
    mine_a = mine_a.reshape(rows, -1)
    mine_b = jnp.where(encoder, mine_a, mine_b.reshape(rows, -1))
    grad_a = left_product(mine_a, grad_first.reshape(rows, -1))
    grad_b = left_product(mine_b, grad_second.reshape(rows, -1))
    bands = []
    for b in range(m):
        band = landed[0]
        for j in range(1, m):
            band = jnp.where(col == (b + j) % m, landed[j], band)
        bands.append(band)
    grad_states = jnp.concatenate(bands, axis=0)
    return (grad_states[None], grad_a[None], grad_b[None])


def packed_ids(lengths, names, tokens):
    n, seqs = lengths.shape
    place = lax.broadcasted_iota(jnp.int32, (n, tokens), 1)
    start = jnp.zeros((n, 1), jnp.int32)
    ids = jnp.zeros((n, tokens), jnp.int32)
    for i in range(seqs):
        length = lengths[:, i : i + 1]
        offset = place - start
        ids = jnp.where((offset >= 0) & (offset < length), names(i), ids)
        start = start + length
    return ids.astype(jnp.float32)


def fused_kernel(
    n, m, x_hbm, cot_hbm, gain, src_len, tgt_len, dest, proj_a, proj_b,
    result, out_a, out_b, mine_a, mine_b,
    x, xall, wbuf, own, other, grad_a, grad_b, id_col, id_row, total, mine, partial, landed,
    in_sem, wsem, loc_sem, out_sem, zx_send, zx_recv, px_send, px_recv, line_send, line_recv,
    sec_send, sec_recv, za_send, za_recv, sl_send, sl_recv, rs_send, rs_recv, ag_send, ag_recv,
):
    me = lax.axis_index("dp")
    col = lax.axis_index("mp")
    sec = lax.axis_index("section")
    encoder = sec == 0
    decoder = sec == 1
    tokens, width = x.shape
    pieces, half = wbuf.shape[1], wbuf.shape[3]
    part = tokens // m
    cols = width // n
    rows = n * tokens
    step = total.shape[1]
    chunks = width // step
    seqs = src_len.shape[1]
    f32, bf16 = jnp.float32, jnp.bfloat16
    spare = lax.rem(me + 1, n)
    near_x = col + 1 - 2 * lax.rem(col, 2)
    near_y = lax.rem(col + 2, m)
    band = pl.ds(pl.multiple_of(col * part, part), part)
    lane = lax.broadcasted_iota(jnp.int32, (1, LANES), 1) // HEAD_DIM
    zero = jnp.zeros((), bf16)

    def remote(src, dst, send, recv, **device):
        return pltpu.make_async_remote_copy(
            src_ref=src, dst_ref=dst, send_sem=send, recv_sem=recv,
            device_id=device, device_id_type=MESH,
        )

    def weight_copy(which, p):
        src = (proj_a, proj_b)[which]
        return pltpu.make_async_copy(
            src.at[0, :, pl.ds(pl.multiple_of(p * half, half), half)],
            wbuf.at[which, p], wsem.at[which, p],
        )

    x_copy = pltpu.make_async_copy(x_hbm.at[0], x, in_sem.at[0])
    cot_copy = pltpu.make_async_copy(cot_hbm, xall.at[spare], in_sem.at[1])
    x_copy.start()
    pl.when(decoder)(cot_copy.start)
    for p in range(pieces):
        for which in (0, 1):
            weight_copy(which, p).start()

    barrier = pltpu.get_barrier_semaphore()
    for j in range(1, n):
        pl.semaphore_signal(
            barrier, inc=1, device_id={"dp": lax.rem(me + j, n)}, device_id_type=MESH
        )
    for j in range(1, m):
        pl.semaphore_signal(
            barrier, inc=1, device_id={"mp": lax.rem(col + j, m)}, device_id_type=MESH
        )
    pl.semaphore_signal(barrier, inc=1, device_id={"section": 1 - sec}, device_id_type=MESH)
    pl.semaphore_wait(barrier, n + m - 1)

    def source(way, s):
        return me - (1 - 2 * way) * (1 + s)

    def got(way, s):
        src = source(way, s)
        return jnp.logical_and(src >= 0, src < n)

    def line_ok(way, s):
        chunk = source(way, s - 1)
        target = me + 1 - 2 * way
        inside = jnp.logical_and(chunk >= 0, chunk < n)
        return jnp.logical_and(inside, jnp.logical_and(target >= 0, target < n))

    def zx_copy(way, s):
        ref = xall.at[source(way, s - 1), band, :]
        return remote(ref, ref, zx_send.at[way, s], zx_recv.at[way, s], dp=me + 1 - 2 * way)

    def line_copy(way, s, p):
        ref = own.at[p, source(way, s - 1)]
        return remote(
            ref, ref, line_send.at[way, s, p], line_recv.at[way, s, p], dp=me + 1 - 2 * way
        )

    def sec_copy(chunk, p):
        return remote(
            own.at[p, chunk], other.at[p, chunk],
            sec_send.at[chunk, p], sec_recv.at[chunk, p], section=1 - sec,
        )

    def plane(view, send, recv, kind):
        small = part // 2
        start = (col * part, col * part, near_x * part, near_y * part + small)[kind]
        size = (part, part, small, small)[kind]
        target = (near_x, near_y, near_y, near_x)[kind]
        ref = view(pl.ds(pl.multiple_of(start, small), size))
        return remote(ref, ref, send.at[kind], recv.at[kind], mp=target)

    def px_copy(src, kind):
        return plane(
            lambda at: xall.at[src, at, :], px_send.at[src], px_recv.at[src], kind
        )

    def za_copy(which, j):
        peer = lax.rem(me + j, n)
        src = xall.at[(me, spare)[which]]
        return remote(
            src.at[band, pl.ds(pl.multiple_of(peer * cols, cols), cols)],
            (mine_a, mine_b)[which].at[me, band, :],
            za_send.at[which, j], za_recv.at[which, j], dp=peer,
        )

    def sl_copy(which, j, kind):
        block = lax.rem(me + n - j, n)
        return plane(
            lambda at: (mine_a, mine_b)[which].at[block, at, :],
            sl_send.at[which, j], sl_recv.at[which, j], kind,
        )

    def scatter(j, d):
        peer = lax.rem(col + j, m)
        at = pl.ds(pl.multiple_of(d * step, step), step)
        return remote(
            partial.at[pl.ds(pl.multiple_of(peer * part, part), part), at],
            landed.at[j, :, at], rs_send.at[j, d], rs_recv.at[j, d], mp=peer,
        )

    def gather(j):
        return remote(
            result.at[band, :], result.at[band, :],
            ag_send.at[j], ag_recv.at[j], mp=lax.rem(col + j, m),
        )

    my_cols = pl.ds(pl.multiple_of(me * cols, cols), cols)

    def keep_slice(which):
        src = xall.at[(me, spare)[which]]
        return pltpu.make_async_copy(
            src.at[:, my_cols], (mine_a, mine_b)[which].at[me], loc_sem.at[which]
        )

    def keep_all(which):
        return pltpu.make_async_copy(
            xall.at[:, :, my_cols], (mine_a, mine_b)[which], loc_sem.at[which]
        )

    def grad_out(which):
        return pltpu.make_async_copy(
            (grad_a, grad_b)[which], (out_a, out_b)[which], out_sem.at[which]
        )

    @pl.when(decoder)
    def _():
        cot_copy.wait()
        for j in range(1, n):
            za_copy(1, j).start()
        keep_slice(1).start()

    x_copy.wait()
    group = min(tokens, 16)

    @pl.loop(0, tokens // group)
    def _(r):
        at = pl.ds(pl.multiple_of(r * group, group), group)
        xf = x[at, :].astype(f32)
        scale = lax.rsqrt(jnp.mean(xf * xf, axis=-1, keepdims=True) + EPS)
        xall[me, at, :] = (xf * scale * gain[...]).astype(bf16)

    @pl.when(encoder)
    def _():
        for way in (0, 1):
            pl.when(line_ok(way, 0))(lambda way=way: zx_copy(way, 0).start())

    @pl.when(decoder)
    def _():
        for j in range(1, n):
            za_copy(0, j).start()
        keep_slice(0).start()

    src_ids = packed_ids(src_len, lambda i: dest[:, i : i + 1], tokens)
    device = lax.broadcasted_iota(jnp.int32, (n, 1), 0)
    tgt_ids = packed_ids(tgt_len, lambda i: device * seqs + i, tokens)
    id_row[...] = jnp.where(encoder, tgt_ids, src_ids)
    near_ids = jnp.where(encoder, src_ids, tgt_ids)
    for b in range(n):
        id_col[b] = jnp.transpose(jnp.broadcast_to(near_ids[b : b + 1, :], (LANES, tokens)))

    def project(p, blk_a, blk_b, out):
        for which in (0, 1):
            own[p, out, :, which * half : (which + 1) * half] = jnp.dot(
                xall[(blk_a, blk_b)[which]], wbuf[which, p], preferred_element_type=f32
            ).astype(bf16)
        sec_copy(out, p).start()

    def x_line(s):
        for way in (0, 1):

            @pl.when(got(way, s))
            def _():
                zx_copy(way, s).wait_recv()
                pl.when(line_ok(way, s + 1))(lambda: zx_copy(way, s + 1).start())
                px_copy(source(way, s), 0).start()
                px_copy(source(way, s), 1).start()

    def x_near(s):
        for way in (0, 1):

            @pl.when(got(way, s))
            def _():
                src = source(way, s)
                px_copy(src, 0).wait_recv()
                px_copy(src, 2).start()
                px_copy(src, 1).wait_recv()
                px_copy(src, 3).start()

    @pl.loop(0, pieces)
    def _(p):
        for which in (0, 1):
            weight_copy(which, p).wait()
        project(p, me, lax.rem(me + sec, n), me)

        @pl.when(decoder)
        def _():
            for way in (0, 1):
                pl.when(line_ok(way, 0))(lambda way=way: line_copy(way, 0, p).start())

        pl.when(jnp.logical_and(encoder, p == pieces // 2))(lambda: x_line(0))

    def unit(axis, p, blk):
        @pl.loop(0, half // LANES)
        def _(c):
            lo = pl.ds(pl.multiple_of(c * LANES, LANES), LANES)
            hi = pl.ds(pl.multiple_of(half + c * LANES, LANES), LANES)
            at = pl.ds(pl.multiple_of(p * half + c * LANES, LANES), LANES)
            near_a, near_b = own[p, blk, :, lo], own[p, blk, :, hi]
            far_a = other[p, :, :, lo].reshape(rows, LANES)
            far_b = other[p, :, :, hi].reshape(rows, LANES)
            ids = id_col[blk]
            mask = jnp.concatenate([ids == id_row[b : b + 1, :] for b in range(n)], axis=1)
            sum_a, sum_b = None, None
            for h in range(LANES // HEAD_DIM):
                fa = jnp.where(lane == h, far_a, zero)
                fb = jnp.where(lane == h, far_b, zero)
                expo = jnp.exp(jnp.where(mask, right_product(near_a, fa), -jnp.inf))
                norm = jnp.sum(expo, axis=axis, keepdims=True)
                weight = expo * (1.0 / jnp.where(norm == 0.0, 1.0, norm))
                dweight = right_product(near_b, fb)
                shift = jnp.sum(weight * dweight, axis=axis, keepdims=True)
                dscore = (weight * (dweight - shift)).astype(bf16)
                pa = jnp.dot(dscore, fa, preferred_element_type=f32)
                pb = jnp.dot(weight.astype(bf16), fb, preferred_element_type=f32)
                sum_a = pa if sum_a is None else sum_a + pa
                sum_b = pb if sum_b is None else sum_b + pb
            grad_a[blk, :, at] = sum_a.astype(bf16)
            grad_b[blk, :, at] = sum_b.astype(bf16)

    def others(axis, p):
        @pl.loop(1, n)
        def _(j):
            unit(axis, p, lax.rem(me + j, n))

    def ready(p):
        for c in range(n):
            sec_copy(c, p).wait_recv()

    def reduce_own(which_all):
        @pl.loop(0, chunks)
        def _(d):
            at = pl.ds(pl.multiple_of(d * step, step), step)
            acc = None
            for which in which_all:
                for p in range(pieces):
                    left = (grad_a, grad_b)[which][me, :, p * half : (p + 1) * half]
                    term = right_product(left, wbuf[which, p, at, :])
                    acc = term if acc is None else acc + term
            total[...] = acc
            partial[:, at] = acc.astype(bf16)
            mine[:, at] = total[band, :]
            for j in range(1, m):
                scatter(j, d).start()

    def finish_own():
        xf = x[band, :].astype(f32)
        scale = lax.rsqrt(jnp.mean(xf * xf, axis=-1, keepdims=True) + EPS)
        for j in range(1, m):
            for d in range(chunks):
                scatter(j, d).wait_recv()
        dnorm = mine[...]
        for j in range(1, m):
            dnorm = dnorm + landed[j].astype(f32)
        upper = gain[...] * dnorm
        inner = jnp.mean(xf * upper, axis=-1, keepdims=True)
        result[band, :] = (scale * upper - xf * scale * scale * scale * inner).astype(bf16)
        for j in range(1, m):
            gather(j).start()

    def wave(w):
        for s in range(max(0, w - pieces + 1), min(n - 1, w + 1)):
            p = w - s
            for way in (0, 1):

                @pl.when(got(way, s))
                def _():
                    line_copy(way, s, p).wait_recv()
                    if s + 1 < n - 1:
                        pl.when(line_ok(way, s + 1))(
                            lambda: line_copy(way, s + 1, p).start()
                        )
                    sec_copy(source(way, s), p).start()

    @pl.when(encoder)
    def _():
        @pl.loop(0, n)
        def _(t):
            pl.when(t < n - 2)(lambda: x_line(t + 1))
            pl.when(t < n - 1)(lambda: x_near(t))

            @pl.when(t >= 1)
            def _():
                @pl.loop(0, 2)
                def _(way):
                    @pl.when(got(way, t - 1))
                    def _():
                        src = source(way, t - 1)
                        px_copy(src, 2).wait_recv()
                        px_copy(src, 3).wait_recv()
                        pl.loop(0, pieces)(lambda p: project(p, src, src, src))

        for which in (0, 1):
            keep_all(which).start()

        @pl.loop(0, pieces)
        def _(p):
            ready(p)
            unit(0, p, me)
            pl.when(jnp.logical_and(p >= 1, p < pieces - 1))(lambda: others(0, p - 1))

        reduce_own((0, 1))
        pl.loop(pieces - 2, pieces)(lambda p: others(0, p))
        for which in (0, 1):
            grad_out(which).start()
        finish_own()
        for way in (0, 1):
            for s in range(n - 1):
                pl.when(line_ok(way, s))(lambda way=way, s=s: zx_copy(way, s).wait_send())

                @pl.when(got(way, s))
                def _():
                    for kind in range(4):
                        px_copy(source(way, s), kind).wait_send()
        for which in (0, 1):
            keep_all(which).wait()

    @pl.when(decoder)
    def _():
        for w in range(pieces):
            wave(w)
        for which in (0, 1):
            for j in range(1, n):
                za_copy(which, j).wait_recv()
                for kind in (0, 1):
                    sl_copy(which, j, kind).start()

        @pl.loop(0, pieces)
        def _(p):
            ready(p)
            unit(1, p, me)

        reduce_own((0,))
        for which in (0, 1):
            for j in range(1, n):
                for kind in (0, 1):
                    sl_copy(which, j, kind).wait_recv()
                    sl_copy(which, j, 2 + kind).start()
        for w in range(pieces, pieces + n - 2):
            wave(w)

        @pl.loop(0, pieces)
        def _(p):
            others(1, p)
            pl.when(p == 1)(finish_own)

        for which in (0, 1):
            grad_out(which).start()
        for which in (0, 1):
            keep_slice(which).wait()
            for j in range(1, n):
                za_copy(which, j).wait_send()
                for kind in range(4):
                    sl_copy(which, j, kind).wait_send()
                for kind in (2, 3):
                    sl_copy(which, j, kind).wait_recv()
        for p in range(pieces):
            for s in range(n - 1):
                for way in (0, 1):
                    pl.when(line_ok(way, s))(
                        lambda way=way, s=s, p=p: line_copy(way, s, p).wait_send()
                    )

    for p in range(pieces):
        for c in range(n):
            sec_copy(c, p).wait_send()
    for j in range(1, m):
        for d in range(chunks):
            scatter(j, d).wait_send()
        gather(j).wait()
    for which in (0, 1):
        grad_out(which).wait()


def fused_scratch(n, m, tokens, width, inner, half, step):
    pieces = inner // half
    part = tokens // m
    chunks = width // step
    dma = pltpu.SemaphoreType.DMA
    vmem = pltpu.VMEM
    bf16, f32 = jnp.bfloat16, jnp.float32
    buffers = [
        vmem((tokens, width), bf16), vmem((n, tokens, width), bf16),
        vmem((2, pieces, width, half), bf16),
        vmem((pieces, n, tokens, 2 * half), bf16), vmem((pieces, n, tokens, 2 * half), bf16),
        vmem((n, tokens, inner), bf16), vmem((n, tokens, inner), bf16),
        vmem((n, tokens, LANES), f32), vmem((n, tokens), f32),
        vmem((tokens, step), f32), vmem((part, width), f32),
        vmem((tokens, width), bf16), vmem((m, part, width), bf16),
    ]
    pair = lambda *shape: [dma(shape), dma(shape)]
    sems = [dma((2,)), dma((2, pieces)), dma((2,)), dma((2,))]
    sems += pair(2, n) + pair(n, 4) + pair(2, n, pieces) + pair(n, pieces)
    sems += pair(2, n) + pair(2, n, 4) + pair(m, chunks) + pair(m)
    return buffers, sems


def fused_fits(n, m, tokens, width, inner):
    if m != 4 or n < 2 or tokens != LANES or inner < 4 * LANES:
        return False
    buffers, _ = fused_scratch(n, m, tokens, width, inner, 2 * LANES, 4 * LANES)
    size = 0
    for buffer in buffers:
        count = jnp.dtype(buffer.dtype).itemsize
        for extent in buffer.shape:
            count *= extent
        size += count
    return size + tokens * width * 2 < 48 * 2**20


def fused(n, m, states, gains, proj_a, proj_b, cotangent, src_len, tgt_len, dest):
    _, tokens, width = states.shape
    inner = proj_a.shape[2]
    buffers, sems = fused_scratch(n, m, tokens, width, inner, 2 * LANES, 4 * LANES)
    bf16 = jnp.bfloat16
    grad = jax.ShapeDtypeStruct((n, tokens, inner), bf16)
    slices = jax.ShapeDtypeStruct((n, tokens, width // n), bf16)
    vmem = pl.BlockSpec(memory_space=pltpu.VMEM)
    hbm = pl.BlockSpec(memory_space=pltpu.HBM)
    return pl.pallas_call(
        functools.partial(fused_kernel, n, m),
        out_shape=(jax.ShapeDtypeStruct((tokens, width), bf16), grad, grad, slices, slices),
        in_specs=[hbm, hbm, vmem, vmem, vmem, vmem, hbm, hbm],
        out_specs=[vmem, hbm, hbm, hbm, hbm],
        scratch_shapes=buffers + sems,
        compiler_params=pltpu.CompilerParams(
            collective_id=2, has_side_effects=True, vmem_limit_bytes=56 * 2**20
        ),
        name="fused",
    )(states, cotangent, gains, src_len, tgt_len, dest, proj_a, proj_b)


def per_device(states, gains, proj_a, proj_b, cotangent, src_len, tgt_len, dest):
    n = lax.axis_size("dp")
    m = lax.axis_size("mp")
    _, tokens, width = states.shape
    inner = proj_a.shape[2]
    args = (states, gains, proj_a, proj_b, cotangent, src_len, tgt_len, dest)
    if not fused_fits(n, m, tokens, width, inner):
        return stepwise(*args)
    result, grad_first, grad_second, mine_a, mine_b = fused(n, m, *args)
    rows = n * tokens
    grad_a = left_product(mine_a.reshape(rows, -1), grad_first.reshape(rows, -1))
    grad_b = left_product(mine_b.reshape(rows, -1), grad_second.reshape(rows, -1))
    return (result[None], grad_a[None], grad_b[None])


def solution(mesh):
    return jax.shard_map(
        per_device,
        mesh=mesh,
        in_specs=(
            P("section", "dp", None),
            P("section", None),
            P("section", None, "mp"),
            P("section", None, "mp"),
            P("dp", None),
            P(),
            P(),
            P(),
        ),
        out_specs=(P("section", "dp", None), P("section", "dp", "mp"), P("section", "dp", "mp")),
        check_vma=False,
    )
```

```python
import functools

import jax
import jax.numpy as jnp
from jax import lax
from jax.experimental import pallas as pl
from jax.experimental.pallas import tpu as pltpu
from jax.sharding import PartitionSpec as P

HEAD_DIM = 64
LANES = 128
EPS = 1e-06
MESH = pl.DeviceIdType.MESH


def rms_forward(states_row, gain):
    xf = states_row.astype(jnp.float32)
    scale = lax.rsqrt(jnp.mean(xf * xf, axis=-1, keepdims=True) + EPS)
    return (xf, scale, (xf * scale * gain).astype(jnp.bfloat16))


def left_product(left, right):
    return lax.dot_general(
        left, right, (((0,), (0,)), ((), ())), preferred_element_type=jnp.float32
    )


def right_product(rows, weight):
    return lax.dot_general(
        rows, weight, (((1,), (1,)), ((), ())), preferred_element_type=jnp.float32
    )


def sequence_of(lengths, names, tokens):
    slot = jnp.arange(lengths.shape[1], dtype=jnp.int32)
    before = slot[:, None] < slot[None, :]
    starts = jnp.sum(jnp.where(before[None], lengths[:, :, None], 0), axis=1)
    place = jnp.arange(tokens, dtype=jnp.int32)[None, :, None]
    offset = place - starts[:, None, :]
    inside = (offset >= 0) & (offset < lengths[:, None, :])
    return jnp.sum(jnp.where(inside, names[:, None, :], 0), axis=-1).reshape(-1)


def attend_piece(encoder, p, group, id_col, id_row, own, other, out_a, out_b, acc_a, acc_b):
    n, tokens, width = own.shape[1:]
    half = width // 2
    rows = n * tokens
    blocks = n // group
    lane = lax.broadcasted_iota(jnp.int32, (1, LANES), 1) // HEAD_DIM
    zero = jnp.zeros((), jnp.bfloat16)
    f32 = jnp.float32

    def cut(ref, which, c, at):
        lo = pl.multiple_of(which * half + c * LANES, LANES)
        return ref[p, at, :, pl.ds(lo, LANES)].reshape(-1, LANES)

    every = pl.ds(0, n)

    @pl.loop(0, half // LANES)
    def _(c):
        out_cols = pl.ds(pl.multiple_of(p * half + c * LANES, LANES), LANES)

        @pl.when(encoder)
        def _():
            keys, values = cut(own, 0, c, every), cut(own, 1, c, every)
            if blocks > 1:
                acc_a[...] = jnp.zeros_like(acc_a)
                acc_b[...] = jnp.zeros_like(acc_b)

            def block(b):
                at = pl.ds(b * group, group)
                query, dout = cut(other, 0, c, at), cut(other, 1, c, at)
                mask = id_col[...].reshape(rows, 1) == id_row[b]
                dk, dv = None, None
                for h in range(LANES // HEAD_DIM):
                    qh = jnp.where(lane == h, query, zero)
                    dh = jnp.where(lane == h, dout, zero)
                    expo = jnp.exp(jnp.where(mask, right_product(keys, qh), -jnp.inf))
                    weight = expo * (1.0 / jnp.sum(expo, axis=0, keepdims=True))
                    dweight = right_product(values, dh)
                    total = jnp.sum(weight * dweight, axis=0, keepdims=True)
                    dscore = (weight * (dweight - total)).astype(jnp.bfloat16)
                    pk = jnp.dot(dscore, qh, preferred_element_type=f32)
                    pv = jnp.dot(weight.astype(jnp.bfloat16), dh, preferred_element_type=f32)
                    dk = pk if dk is None else dk + pk
                    dv = pv if dv is None else dv + pv
                if blocks == 1:
                    out_a[:, :, out_cols] = dk.astype(jnp.bfloat16).reshape(n, tokens, LANES)
                    out_b[:, :, out_cols] = dv.astype(jnp.bfloat16).reshape(n, tokens, LANES)
                else:
                    acc_a[...] += dk
                    acc_b[...] += dv

            if blocks == 1:
                block(0)
            else:
                pl.loop(0, blocks)(block)
                out_a[:, :, out_cols] = acc_a[...].astype(jnp.bfloat16).reshape(n, tokens, LANES)
                out_b[:, :, out_cols] = acc_b[...].astype(jnp.bfloat16).reshape(n, tokens, LANES)

        @pl.when(jnp.logical_not(encoder))
        def _():
            keys, values = cut(other, 0, c, every), cut(other, 1, c, every)

            def block(b):
                at = pl.ds(b * group, group)
                query, dout = cut(own, 0, c, at), cut(own, 1, c, at)
                ids = id_col[at, :, :].reshape(group * tokens, 1)
                mask = None
                dq, att = None, None
                for h in range(LANES // HEAD_DIM):
                    kh = jnp.where(lane == h, keys, zero)
                    vh = jnp.where(lane == h, values, zero)
                    score = right_product(query, kh)
                    if mask is None:
                        span = group * tokens
                        mask = jnp.concatenate(
                            [ids == id_row[i] for i in range(rows // span)], axis=1
                        )
                    expo = jnp.exp(jnp.where(mask, score, -jnp.inf))
                    weight = expo * (1.0 / jnp.sum(expo, axis=1, keepdims=True))
                    dweight = right_product(dout, vh)
                    total = jnp.sum(weight * dweight, axis=1, keepdims=True)
                    dscore = (weight * (dweight - total)).astype(jnp.bfloat16)
                    pq = jnp.dot(dscore, kh, preferred_element_type=f32)
                    pa = jnp.dot(weight.astype(jnp.bfloat16), vh, preferred_element_type=f32)
                    dq = pq if dq is None else dq + pq
                    att = pa if att is None else att + pa
                shape = (group, tokens, LANES)
                out_a[at, :, out_cols] = dq.astype(jnp.bfloat16).reshape(shape)
                out_b[at, :, out_cols] = att.astype(jnp.bfloat16).reshape(shape)

            if blocks == 1:
                block(0)
            else:
                pl.loop(0, blocks)(block)


def forward_kernel(
    n, m, group, normed, second, id_col, id_row, proj_a, proj_b,
    out_a, out_b, mine_a, mine_b,
    wbuf, paired, own, other, acc_a, acc_b, wsem,
    line_send, line_recv, sec_send, sec_recv, za_send, za_recv, mp_send, mp_recv, loc_sem,
):
    me = lax.axis_index("dp")
    col = lax.axis_index("mp")
    sec = lax.axis_index("section")
    tokens, width = normed.shape
    pieces = wbuf.shape[1]
    half = wbuf.shape[3]
    part = tokens // m
    cols = width // n

    def weight_copy(which, p):
        src = (proj_a, proj_b)[which]
        return pltpu.make_async_copy(
            src.at[0, :, pl.ds(p * half, half)], wbuf.at[which, p], wsem.at[which, p]
        )

    for p in range(pieces):
        for which in (0, 1):
            weight_copy(which, p).start()

    barrier = pltpu.get_barrier_semaphore()
    for j in range(1, n):
        pl.semaphore_signal(
            barrier, inc=1, device_id={"dp": lax.rem(me + j, n)}, device_id_type=MESH
        )
    for j in range(1, m):
        pl.semaphore_signal(
            barrier, inc=1, device_id={"mp": lax.rem(col + j, m)}, device_id_type=MESH
        )
    pl.semaphore_signal(barrier, inc=1, device_id={"section": 1 - sec}, device_id_type=MESH)
    pl.semaphore_wait(barrier, n + m - 1)

    band = pl.ds(pl.multiple_of(col * part, part), part)

    def line_copy(way, s, p):
        chunk = me - s if way == 0 else me + s
        target = me + 1 if way == 0 else me - 1
        src = paired.at[p] if s == 0 else own.at[p, chunk]
        return pltpu.make_async_remote_copy(
            src_ref=src, dst_ref=own.at[p, chunk],
            send_sem=line_send.at[way, s, p], recv_sem=line_recv.at[way, s, p],
            device_id={"dp": target}, device_id_type=MESH,
        )

    def line_ok(way, s):
        if way == 0:
            return jnp.logical_and(me - s >= 0, me < n - 1)
        return jnp.logical_and(me + s <= n - 1, me > 0)

    def got(way, s):
        return me - 1 - s >= 0 if way == 0 else me + 1 + s <= n - 1

    def sec_copy(chunk, p, src):
        return pltpu.make_async_remote_copy(
            src_ref=src, dst_ref=other.at[p, chunk],
            send_sem=sec_send.at[chunk, p], recv_sem=sec_recv.at[chunk, p],
            device_id={"section": 1 - sec}, device_id_type=MESH,
        )

    def za_copy(which, j):
        src, dst = ((normed, mine_a), (second, mine_b))[which]
        peer = lax.rem(me + j, n)
        return pltpu.make_async_remote_copy(
            src_ref=src.at[band, pl.ds(pl.multiple_of(peer * cols, cols), cols)],
            dst_ref=dst.at[me, band, :],
            send_sem=za_send.at[which, j], recv_sem=za_recv.at[which, j],
            device_id={"dp": peer}, device_id_type=MESH,
        )

    def mp_copy(which, j):
        dst = (mine_a, mine_b)[which]
        return pltpu.make_async_remote_copy(
            src_ref=dst.at[:, band, :], dst_ref=dst.at[:, band, :],
            send_sem=mp_send.at[which, j], recv_sem=mp_recv.at[which, j],
            device_id={"mp": lax.rem(col + j, m)}, device_id_type=MESH,
        )

    def local(which):
        src, dst = ((normed, mine_a), (second, mine_b))[which]
        return pltpu.make_async_copy(
            src.at[band, pl.ds(pl.multiple_of(me * cols, cols), cols)],
            dst.at[me, band, :], loc_sem.at[which],
        )

    def keep(p):
        return pltpu.make_async_copy(paired.at[p], own.at[p, me], loc_sem.at[2 + p])

    def second_too(fn):
        fn(0)
        pl.when(sec == 1)(lambda: fn(1))

    for j in range(1, n):
        second_too(lambda which: za_copy(which, j).start())
    second_too(lambda which: local(which).start())

    for p in range(pieces):
        for which in (0, 1):
            weight_copy(which, p).wait()
            rows_in = (normed, second)[which]
            paired[p, :, which * half : (which + 1) * half] = jnp.dot(
                rows_in[...], wbuf[which, p], preferred_element_type=jnp.float32
            ).astype(jnp.bfloat16)
        for way in (0, 1):
            pl.when(line_ok(way, 0))(lambda way=way, p=p: line_copy(way, 0, p).start())
        sec_copy(me, p, paired.at[p]).start()
        keep(p).start()

    def spread(which):
        local(which).wait()
        for j in range(1, n):
            za_copy(which, j).wait_recv()
        for j in range(1, m):
            mp_copy(which, j).start()

    second_too(spread)

    for wave in range(pieces + n - 2):
        for s in range(max(0, wave - pieces + 1), min(n - 1, wave + 1)):
            p = wave - s
            for way in (0, 1):

                @pl.when(got(way, s))
                def _():
                    line_copy(way, s, p).wait_recv()
                    chunk = me - 1 - s if way == 0 else me + 1 + s
                    if s + 1 < n - 1:
                        pl.when(line_ok(way, s + 1))(
                            lambda: line_copy(way, s + 1, p).start()
                        )
                    sec_copy(chunk, p, own.at[p, chunk]).start()

        p = wave - (n - 2)
        if p >= 0:
            keep(p).wait()
            for c in range(n):
                sec_copy(c, p, own.at[p, c]).wait_recv()
            attend_piece(
                sec == 0, p, group, id_col, id_row, own, other, out_a, out_b, acc_a, acc_b
            )

    def finish(which):
        for j in range(1, n):
            za_copy(which, j).wait_send()
        for j in range(1, m):
            mp_copy(which, j).wait()

    second_too(finish)
    for p in range(pieces):
        for s in range(n - 1):
            for way in (0, 1):
                pl.when(line_ok(way, s))(
                    lambda way=way, s=s, p=p: line_copy(way, s, p).wait_send()
                )
        for c in range(n):
            sec_copy(c, p, own.at[p, c]).wait_send()


def forward(n, m, normed, second, id_c, id_r, proj_a, proj_b):
    tokens, width = normed.shape
    inner = proj_a.shape[2]
    half = 2 * LANES
    pieces = inner // half
    rows = n * tokens
    group = max(1, min(n, 512 * 512 // (rows * tokens)))
    blocks = n // group
    grad = jax.ShapeDtypeStruct((n, tokens, inner), jnp.bfloat16)
    mine = jax.ShapeDtypeStruct((n, tokens, width // n), jnp.bfloat16)
    acc = (rows, LANES) if blocks > 1 else (8, LANES)
    dma = pltpu.SemaphoreType.DMA
    vmem = pl.BlockSpec(memory_space=pltpu.VMEM)
    anyw = pl.BlockSpec(memory_space=pltpu.HBM)
    bf16 = jnp.bfloat16
    return pl.pallas_call(
        functools.partial(forward_kernel, n, m, group),
        out_shape=(grad, grad, mine, mine),
        in_specs=[vmem] * 4 + [anyw] * 2,
        out_specs=[vmem, vmem, anyw, anyw],
        scratch_shapes=[
            pltpu.VMEM((2, pieces, width, half), bf16),
            pltpu.VMEM((pieces, tokens, 2 * half), bf16),
            pltpu.VMEM((pieces, n, tokens, 2 * half), bf16),
            pltpu.VMEM((pieces, n, tokens, 2 * half), bf16),
            pltpu.VMEM(acc, jnp.float32), pltpu.VMEM(acc, jnp.float32),
            dma((2, pieces)),
            dma((2, n, pieces)), dma((2, n, pieces)), dma((n, pieces)), dma((n, pieces)),
            dma((2, n)), dma((2, n)), dma((2, m)), dma((2, m)), dma((2 + pieces,)),
        ],
        compiler_params=pltpu.CompilerParams(
            collective_id=0, has_side_effects=True, vmem_limit_bytes=67000000
        ),
        name="forward",
    )(normed, second, id_c.reshape(n, tokens, 1), id_r.reshape(blocks, 1, rows // blocks),
      proj_a, proj_b)


def reduce_kernel(
    m, grad_a, grad_b, proj_a, proj_b, x_ref, gain_ref, result,
    left, wbuf, total, mine, partial, landed, gsem, wsem, send, recv,
):
    me = lax.axis_index("dp")
    col = lax.axis_index("mp")
    encoder = lax.axis_index("section") == 0
    tokens = x_ref.shape[0]
    part = tokens // m
    chunks, step = wbuf.shape[1:3]

    def left_copy(which):
        return pltpu.make_async_copy(
            (grad_a, grad_b)[which].at[me], left.at[which], gsem.at[which]
        )

    def weight_copy(which, c):
        return pltpu.make_async_copy(
            (proj_a, proj_b)[which].at[0, pl.ds(c * step, step), :],
            wbuf.at[which, c], wsem.at[which, c],
        )

    left_copy(0).start()
    pl.when(encoder)(lambda: left_copy(1).start())
    for c in range(chunks):
        weight_copy(0, c).start()
        pl.when(encoder)(lambda c=c: weight_copy(1, c).start())

    barrier = pltpu.get_barrier_semaphore()
    for j in range(1, m):
        pl.semaphore_signal(
            barrier, inc=1, device_id={"mp": lax.rem(col + j, m)}, device_id_type=MESH
        )
    pl.semaphore_wait(barrier, m - 1)

    def scatter(j, c):
        peer = lax.rem(col + j, m)
        rows = pl.ds(pl.multiple_of(peer * part, part), part)
        at = pl.ds(c * step, step)
        return pltpu.make_async_remote_copy(
            src_ref=partial.at[rows, at], dst_ref=landed.at[j, :, at],
            send_sem=send.at[j, c], recv_sem=recv.at[j, c],
            device_id={"mp": peer}, device_id_type=MESH,
        )

    band = pl.ds(pl.multiple_of(col * part, part), part)
    left_copy(0).wait()
    pl.when(encoder)(lambda: left_copy(1).wait())
    for c in range(chunks):
        weight_copy(0, c).wait()
        total[...] = right_product(left[0], wbuf[0, c])

        @pl.when(encoder)
        def _():
            weight_copy(1, c).wait()
            total[...] += right_product(left[1], wbuf[1, c])

        partial[:, c * step : (c + 1) * step] = total[...].astype(jnp.bfloat16)
        mine[:, c * step : (c + 1) * step] = total[band, :]
        for j in range(1, m):
            scatter(j, c).start()
    x = x_ref[band, :].astype(jnp.float32)
    scale = lax.rsqrt(jnp.mean(x * x, axis=-1, keepdims=True) + EPS)
    for j in range(1, m):
        for c in range(chunks):
            scatter(j, c).wait_recv()
    dnorm = mine[...]
    for j in range(1, m):
        dnorm = dnorm + landed[j].astype(jnp.float32)
    upper = gain_ref[...] * dnorm
    inner = jnp.mean(x * upper, axis=-1, keepdims=True)
    result[...] = (scale * upper - x * scale * scale * scale * inner).astype(jnp.bfloat16)
    for j in range(1, m):
        for c in range(chunks):
            scatter(j, c).wait_send()


def reduce_norm(m, grad_a, grad_b, proj_a, proj_b, states, gain):
    tokens, width = states.shape
    inner = proj_a.shape[2]
    part = tokens // m
    step = 4 * LANES
    chunks = width // step
    dma = pltpu.SemaphoreType.DMA
    bf16, f32 = jnp.bfloat16, jnp.float32
    vmem = pl.BlockSpec(memory_space=pltpu.VMEM)
    return pl.pallas_call(
        functools.partial(reduce_kernel, m),
        out_shape=jax.ShapeDtypeStruct((part, width), bf16),
        in_specs=[pl.BlockSpec(memory_space=pltpu.HBM)] * 4 + [vmem] * 2,
        out_specs=vmem,
        scratch_shapes=[
            pltpu.VMEM((2, tokens, inner), bf16),
            pltpu.VMEM((2, chunks, step, inner), bf16),
            pltpu.VMEM((tokens, step), f32),
            pltpu.VMEM((part, width), f32),
            pltpu.VMEM((tokens, width), bf16),
            pltpu.VMEM((m, part, width), bf16),
            dma((2,)), dma((2, chunks)), dma((m, chunks)), dma((m, chunks)),
        ],
        compiler_params=pltpu.CompilerParams(
            collective_id=1, has_side_effects=True, vmem_limit_bytes=66500000
        ),
        name="reduce_norm",
    )(grad_a, grad_b, proj_a, proj_b, states, gain)


def stepwise(states, gains, proj_a, proj_b, cotangent, src_len, tgt_len, dest):
    encoder = lax.axis_index("section") == 0
    member = lax.axis_index("dp")
    n = lax.axis_size("dp")
    m = lax.axis_size("mp")
    gain = gains[0]
    weight_a = proj_a[0]
    weight_b = proj_b[0]
    tokens = states.shape[1]
    _, _, normed = rms_forward(states[0], gain)
    second_left = jnp.where(encoder, normed, cotangent)
    rows = n * tokens
    seqs = tgt_len.shape[1]
    names = jnp.arange(n * seqs, dtype=jnp.int32).reshape(n, seqs)
    id_c = sequence_of(
        jnp.where(encoder, src_len, tgt_len), jnp.where(encoder, dest, names), tokens
    )
    id_r = sequence_of(
        jnp.where(encoder, tgt_len, src_len), jnp.where(encoder, names, dest), tokens
    )
    grad_first, grad_second, mine_a, mine_b = forward(
        n, m, normed, second_left, id_c, id_r, proj_a, proj_b
    )
    mine = reduce_norm(m, grad_first, grad_second, proj_a, proj_b, states[0], gains)
    col = lax.axis_index("mp")
    landed = [mine] + [
        lax.ppermute(mine, "mp", [(i, (i + j) % m) for i in range(m)]) for j in range(1, m)
    ]
    mine_a = mine_a.reshape(rows, -1)
    mine_b = jnp.where(encoder, mine_a, mine_b.reshape(rows, -1))
    grad_a = left_product(mine_a, grad_first.reshape(rows, -1))
    grad_b = left_product(mine_b, grad_second.reshape(rows, -1))
    bands = []
    for b in range(m):
        band = landed[0]
        for j in range(1, m):
            band = jnp.where(col == (b + j) % m, landed[j], band)
        bands.append(band)
    grad_states = jnp.concatenate(bands, axis=0)
    return (grad_states[None], grad_a[None], grad_b[None])


def packed_ids(lengths, names, tokens):
    n, seqs = lengths.shape
    place = lax.broadcasted_iota(jnp.int32, (n, tokens), 1)
    start = jnp.zeros((n, 1), jnp.int32)
    ids = jnp.zeros((n, tokens), jnp.int32)
    for i in range(seqs):
        length = lengths[:, i : i + 1]
        offset = place - start
        ids = jnp.where((offset >= 0) & (offset < length), names(i), ids)
        start = start + length
    return ids.astype(jnp.float32)


def fused_kernel(
    n, m, x_hbm, cot_hbm, gain_hbm, src_hbm, tgt_hbm, dest_hbm, proj_a, proj_b,
    result, out_a, out_b, mine_a, mine_b,
    gain, src_len, tgt_len, dest, rest, x, xall, wbuf, own, other, grad_a, grad_b, id_col, id_row, total, partial, landed,
    gate, in_sem, wsem, loc_sem, out_sem, zx_send, zx_recv, px_send, px_recv, line_send, line_recv,
    sec_send, sec_recv, za_send, za_recv, sl_send, sl_recv, rs_send, rs_recv, ag_send, ag_recv,
):
    me = lax.axis_index("dp")
    col = lax.axis_index("mp")
    sec = lax.axis_index("section")
    encoder = sec == 0
    decoder = sec == 1
    tokens, width = x.shape
    pieces, half = wbuf.shape[1], wbuf.shape[3]
    part = tokens // m
    cols = width // n
    rows = n * tokens
    chunks = rs_send.shape[1]
    step = width // chunks
    quarter = width // pieces
    hops = (n - 1) * pieces
    seqs = src_len.shape[1]
    f32, bf16 = jnp.float32, jnp.bfloat16
    spare = lax.rem(me + 1, n)
    near_x = col + 1 - 2 * lax.rem(col, 2)
    near_y = lax.rem(col + 2, m)
    band = pl.ds(pl.multiple_of(col * part, part), part)
    lane = lax.broadcasted_iota(jnp.int32, (1, LANES), 1) // HEAD_DIM
    zero = jnp.zeros((), bf16)

    def remote(src, dst, send, recv, **device):
        return pltpu.make_async_remote_copy(
            src_ref=src, dst_ref=dst, send_sem=send, recv_sem=recv,
            device_id=device, device_id_type=MESH,
        )

    def weight_copy(which, p):
        src = (proj_a, proj_b)[which]
        return pltpu.make_async_copy(
            src.at[0, :, pl.ds(pl.multiple_of(p * half, half), half)],
            wbuf.at[which, p], wsem.at[which, p],
        )

    x_copy = pltpu.make_async_copy(x_hbm.at[0], x, in_sem.at[0])
    cot_copy = pltpu.make_async_copy(cot_hbm, xall.at[spare], in_sem.at[1])
    small_copies = [
        pltpu.make_async_copy(src, dst, in_sem.at[2 + i])
        for i, (src, dst) in enumerate(
            ((gain_hbm, gain), (src_hbm, src_len), (tgt_hbm, tgt_len), (dest_hbm, dest))
        )
    ]
    x_copy.start()
    for copy in small_copies:
        copy.start()
    pl.when(decoder)(cot_copy.start)
    for p in range(pieces):
        for which in (0, 1):
            weight_copy(which, p).start()

    barrier = pltpu.get_barrier_semaphore()
    for j in range(1, n):
        pl.semaphore_signal(
            barrier, inc=1, device_id={"dp": lax.rem(me + j, n)}, device_id_type=MESH
        )
    for j in range(1, m):
        pl.semaphore_signal(
            barrier, inc=1, device_id={"mp": lax.rem(col + j, m)}, device_id_type=MESH
        )
    pl.semaphore_signal(barrier, inc=1, device_id={"section": 1 - sec}, device_id_type=MESH)
    pl.semaphore_wait(barrier, n + m - 1)

    def source(way, s):
        return me - (1 - 2 * way) * (1 + s)

    def got(way, s):
        src = source(way, s)
        return jnp.logical_and(src >= 0, src < n)

    def line_ok(way, s):
        chunk = source(way, s - 1)
        target = me + 1 - 2 * way
        inside = jnp.logical_and(chunk >= 0, chunk < n)
        return jnp.logical_and(inside, jnp.logical_and(target >= 0, target < n))

    def span(q):
        return pl.ds(pl.multiple_of(q * quarter, quarter), quarter)

    def zx_copy(way, s, q):
        ref = xall.at[source(way, s - 1), band, span(q)]
        return remote(
            ref, ref, zx_send.at[way, s, q], zx_recv.at[way, s, q], dp=me + 1 - 2 * way
        )

    def line_copy(way, s, p):
        ref = own.at[p, source(way, s - 1)]
        return remote(
            ref, ref, line_send.at[way, s, p], line_recv.at[way, s, p], dp=me + 1 - 2 * way
        )

    def sec_copy(chunk, p):
        return remote(
            own.at[p, chunk], other.at[p, chunk],
            sec_send.at[chunk, p], sec_recv.at[chunk, p], section=1 - sec,
        )

    def plane(view, send, recv, kind):
        small = part // 2
        start = (col * part, col * part, near_x * part, near_y * part + small)[kind]
        size = (part, part, small, small)[kind]
        target = (near_x, near_y, near_y, near_x)[kind]
        ref = view(pl.ds(pl.multiple_of(start, small), size))
        return remote(ref, ref, send.at[kind], recv.at[kind], mp=target)

    def px_copy(src, q, kind):
        return plane(
            lambda at: xall.at[src, at, span(q)], px_send.at[src, q], px_recv.at[src, q], kind
        )

    def za_copy(which, j):
        peer = lax.rem(me + j, n)
        src = xall.at[(me, spare)[which]]
        return remote(
            src.at[band, pl.ds(pl.multiple_of(peer * cols, cols), cols)],
            (mine_a, mine_b)[which].at[me, band, :],
            za_send.at[which, j], za_recv.at[which, j], dp=peer,
        )

    def sl_copy(which, j, kind):
        block = lax.rem(me + n - j, n)
        return plane(
            lambda at: (mine_a, mine_b)[which].at[block, at, :],
            sl_send.at[which, j], sl_recv.at[which, j], kind,
        )

    def scatter(j, d):
        peer = lax.rem(col + j, m)
        at = pl.ds(pl.multiple_of(d * step, step), step)
        return remote(
            partial.at[pl.ds(pl.multiple_of(peer * part, part), part), at],
            landed.at[j, :, at], rs_send.at[j, d], rs_recv.at[j, d], mp=peer,
        )

    def gather(kind):
        if kind > 1:
            return plane(lambda at: result.at[at, :], ag_send, ag_recv, kind)
        return remote(
            rest, result.at[band, :], ag_send.at[kind], ag_recv.at[kind],
            mp=(near_x, near_y)[kind],
        )

    keep_rest = pltpu.make_async_copy(rest, result.at[band, :], loc_sem.at[2])

    my_cols = pl.ds(pl.multiple_of(me * cols, cols), cols)

    def keep_slice(which):
        src = xall.at[(me, spare)[which]]
        return pltpu.make_async_copy(
            src.at[:, my_cols], (mine_a, mine_b)[which].at[me], loc_sem.at[which]
        )

    def keep_all(which):
        return pltpu.make_async_copy(
            xall.at[:, :, my_cols], (mine_a, mine_b)[which], loc_sem.at[which]
        )

    def grad_out(which):
        return pltpu.make_async_copy(
            (grad_a, grad_b)[which], (out_a, out_b)[which], out_sem.at[which]
        )

    @pl.when(decoder)
    def _():
        cot_copy.wait()
        for j in range(1, n):
            za_copy(1, j).start()

    x_copy.wait()
    for copy in small_copies:
        copy.wait()
    group = min(tokens, 16)

    @pl.loop(0, tokens // group)
    def _(r):
        at = pl.ds(pl.multiple_of(r * group, group), group)
        xf = x[at, :].astype(f32)
        scale = lax.rsqrt(jnp.mean(xf * xf, axis=-1, keepdims=True) + EPS)
        xall[me, at, :] = (xf * scale * gain[...]).astype(bf16)

    @pl.when(encoder)
    def _():
        for q in range(pieces):
            for way in (0, 1):
                pl.when(line_ok(way, 0))(lambda way=way, q=q: zx_copy(way, 0, q).start())

    @pl.when(decoder)
    def _():
        for j in range(1, n):
            za_copy(0, j).start()
        for which in (0, 1):
            keep_slice(which).start()

    src_ids = packed_ids(src_len, lambda i: dest[:, i : i + 1], tokens)
    device = lax.broadcasted_iota(jnp.int32, (n, 1), 0)
    tgt_ids = packed_ids(tgt_len, lambda i: device * seqs + i, tokens)
    id_row[...] = jnp.where(encoder, tgt_ids, src_ids)
    near_ids = jnp.where(encoder, src_ids, tgt_ids)
    for b in range(n):
        id_col[b] = jnp.transpose(jnp.broadcast_to(near_ids[b : b + 1, :], (LANES, tokens)))

    def project(p, blk_a, blk_b, out):
        for which in (0, 1):
            own[p, out, :, which * half : (which + 1) * half] = jnp.dot(
                xall[(blk_a, blk_b)[which]], wbuf[which, p], preferred_element_type=f32
            ).astype(bf16)
        sec_copy(out, p).start()

    def x_line(i):
        s, q = i // pieces, i % pieces
        for way in (0, 1):

            @pl.when(got(way, s))
            def _():
                zx_copy(way, s, q).wait_recv()
                pl.when(line_ok(way, s + 1))(lambda: zx_copy(way, s + 1, q).start())
                for kind in (0, 1):
                    px_copy(source(way, s), q, kind).start()

    def x_near(i):
        s, q = i // pieces, i % pieces
        for way in (0, 1):

            @pl.when(got(way, s))
            def _():
                for kind in (0, 1):
                    px_copy(source(way, s), q, kind).wait_recv()
                    px_copy(source(way, s), q, 2 + kind).start()

    def x_done(i):
        s, q = i // pieces, i % pieces
        for way in (0, 1):

            @pl.when(got(way, s))
            def _():
                for kind in (2, 3):
                    px_copy(source(way, s), q, kind).wait_recv()

    def x_work(i):
        @pl.loop(0, 2)
        def _(way):
            src = source(way, i // pieces)
            pl.when(got(way, i // pieces))(lambda: project(i % pieces, src, src, src))

    @pl.loop(0, pieces)
    def _(p):
        for which in (0, 1):
            weight_copy(which, p).wait()
        project(p, me, lax.rem(me + sec, n), me)

    def unit(axis, p, blk):
        @pl.loop(0, half // LANES, unroll=True)
        def _(c):
            lo = pl.ds(pl.multiple_of(c * LANES, LANES), LANES)
            hi = pl.ds(pl.multiple_of(half + c * LANES, LANES), LANES)
            at = pl.ds(pl.multiple_of(p * half + c * LANES, LANES), LANES)
            near_a, near_b = own[p, blk, :, lo], own[p, blk, :, hi]
            far_a = other[p, :, :, lo].reshape(rows, LANES)
            far_b = other[p, :, :, hi].reshape(rows, LANES)
            ids = id_col[blk]
            mask = jnp.concatenate([ids == id_row[b : b + 1, :] for b in range(n)], axis=1)
            sum_a, sum_b = None, None
            for h in range(LANES // HEAD_DIM):
                fa = jnp.where(lane == h, far_a, zero)
                fb = jnp.where(lane == h, far_b, zero)
                expo = jnp.exp(jnp.where(mask, right_product(near_a, fa), -jnp.inf))
                norm = jnp.sum(expo, axis=axis, keepdims=True)
                weight = expo * (1.0 / jnp.where(norm == 0.0, 1.0, norm))
                dweight = right_product(near_b, fb)
                shift = jnp.sum(weight * dweight, axis=axis, keepdims=True)
                dscore = (weight * (dweight - shift)).astype(bf16)
                pa = jnp.dot(dscore, fa, preferred_element_type=f32)
                pb = jnp.dot(weight.astype(bf16), fb, preferred_element_type=f32)
                sum_a = pa if sum_a is None else sum_a + pa
                sum_b = pb if sum_b is None else sum_b + pb
            grad_a[blk, :, at] = sum_a.astype(bf16)
            grad_b[blk, :, at] = sum_b.astype(bf16)

    def others(axis, p):
        @pl.loop(1, n)
        def _(j):
            unit(axis, p, lax.rem(me + j, n))

    def ready(p):
        for c in range(n):
            sec_copy(c, p).wait_recv()

    def reduce_own(which_all):
        @pl.loop(0, chunks, unroll=2)
        def _(d):
            at = pl.ds(pl.multiple_of(d * step, step), step)
            acc = None
            for which in which_all:
                for p in range(pieces):
                    left = (grad_a, grad_b)[which][me, :, p * half : (p + 1) * half]
                    term = right_product(left, wbuf[which, p, at, :])
                    acc = term if acc is None else acc + term
            total[:, at] = acc
            partial[:, at] = acc.astype(bf16)
            for j in range(1, m):
                scatter(j, d).start()

    def finish_own():
        xf = x[band, :].astype(f32)
        scale = lax.rsqrt(jnp.mean(xf * xf, axis=-1, keepdims=True) + EPS)
        for j in range(1, m):
            for d in range(chunks):
                scatter(j, d).wait_recv()
        dnorm = total[band, :]
        for j in range(1, m):
            dnorm = dnorm + landed[j].astype(f32)
        upper = gain[...] * dnorm
        inner = jnp.mean(xf * upper, axis=-1, keepdims=True)
        rest[...] = (scale * upper - xf * scale * scale * scale * inner).astype(bf16)
        gather(0).start()
        gather(1).start()
        keep_rest.start()

    def relay_own():
        for kind in (0, 1):
            gather(kind).wait_recv()
            gather(2 + kind).start()

    def wave(w):
        for s in range(max(0, w - pieces + 1), min(n - 1, w + 1)):
            p = w - s
            for way in (0, 1):

                @pl.when(got(way, s))
                def _():
                    line_copy(way, s, p).wait_recv()
                    if s + 1 < n - 1:
                        pl.when(line_ok(way, s + 1))(
                            lambda: line_copy(way, s + 1, p).start()
                        )
                    sec_copy(source(way, s), p).start()

    @pl.when(encoder)
    def _():
        lags = (0, 2, 5, 4 + pieces)

        @pl.loop(0, hops + lags[3])
        def _(i):
            for lag, stage in zip(lags, (x_line, x_near, x_done, x_work)):
                at = i - lag
                inside = jnp.logical_and(at >= 0, at < hops)
                pl.when(inside)(lambda stage=stage, at=at: stage(at))

            @pl.when(i == pieces - 1)
            def _():
                pl.semaphore_signal(
                    gate, inc=1, device_id={"section": 1 - sec}, device_id_type=MESH
                )

        for which in (0, 1):
            keep_all(which).start()

        @pl.loop(0, pieces)
        def _(p):
            ready(p)
            unit(0, p, me)

        reduce_own((0, 1))

        @pl.loop(0, pieces)
        def _(p):
            others(0, p)
            pl.when(p == 1)(finish_own)
            pl.when(p == 2)(relay_own)

        for which in (0, 1):
            grad_out(which).start()

        @pl.loop(0, hops)
        def _(i):
            s, q = i // pieces, i % pieces
            for way in (0, 1):
                pl.when(line_ok(way, s))(lambda way=way: zx_copy(way, s, q).wait_send())

                @pl.when(got(way, s))
                def _():
                    for kind in range(4):
                        px_copy(source(way, s), q, kind).wait_send()

        for which in (0, 1):
            keep_all(which).wait()

    @pl.when(decoder)
    def _():
        pl.semaphore_wait(gate, 1)
        for p in range(pieces):
            for way in (0, 1):
                pl.when(line_ok(way, 0))(
                    lambda way=way, p=p: line_copy(way, 0, p).start()
                )
        for w in range(pieces):
            wave(w)
        for which in (0, 1):
            for j in range(1, n):
                za_copy(which, j).wait_recv()
                for kind in (0, 1):
                    sl_copy(which, j, kind).start()

        @pl.loop(0, pieces)
        def _(p):
            ready(p)
            unit(1, p, me)
            for late in range(n - 2):
                pl.when(p == min(late, pieces - 1))(lambda late=late: wave(pieces + late))

        reduce_own((0,))
        for which in (0, 1):
            for j in range(1, n):
                for kind in (0, 1):
                    sl_copy(which, j, kind).wait_recv()
                    sl_copy(which, j, 2 + kind).start()
        @pl.loop(0, pieces)
        def _(p):
            others(1, p)
            pl.when(p == 1)(finish_own)
            pl.when(p == 2)(relay_own)

        for which in (0, 1):
            grad_out(which).start()
        for which in (0, 1):
            keep_slice(which).wait()
            for j in range(1, n):
                za_copy(which, j).wait_send()
                for kind in range(4):
                    sl_copy(which, j, kind).wait_send()
                for kind in (2, 3):
                    sl_copy(which, j, kind).wait_recv()
        for p in range(pieces):
            for s in range(n - 1):
                for way in (0, 1):
                    pl.when(line_ok(way, s))(
                        lambda way=way, s=s, p=p: line_copy(way, s, p).wait_send()
                    )

    for p in range(pieces):
        for c in range(n):
            sec_copy(c, p).wait_send()
    for j in range(1, m):
        for d in range(chunks):
            scatter(j, d).wait_send()
    for kind in range(4):
        gather(kind).wait_send()
    for kind in (2, 3):
        gather(kind).wait_recv()
    keep_rest.wait()
    for which in (0, 1):
        grad_out(which).wait()


def fused_scratch(n, m, seqs, tokens, width, inner, half, step):
    pieces = inner // half
    part = tokens // m
    chunks = width // step
    dma = pltpu.SemaphoreType.DMA
    vmem = pltpu.VMEM
    bf16, f32 = jnp.bfloat16, jnp.float32
    buffers = [
        vmem((1, width), f32), vmem((n, seqs), jnp.int32), vmem((n, seqs), jnp.int32),
        vmem((n, seqs), jnp.int32), vmem((part, width), bf16),
        vmem((tokens, width), bf16), vmem((n, tokens, width), bf16),
        vmem((2, pieces, width, half), bf16),
        vmem((pieces, n, tokens, 2 * half), bf16), vmem((pieces, n, tokens, 2 * half), bf16),
        vmem((n, tokens, inner), bf16), vmem((n, tokens, inner), bf16),
        vmem((n, tokens, LANES), f32), vmem((n, tokens), f32),
        vmem((tokens, width), f32), vmem((tokens, width), bf16), vmem((m, part, width), bf16),
    ]
    pair = lambda *shape: [dma(shape), dma(shape)]
    sems = [pltpu.SemaphoreType.REGULAR, dma((6,)), dma((2, pieces)), dma((3,)), dma((2,))]
    sems += pair(2, n, pieces) + pair(n, pieces, 4) + pair(2, n, pieces) + pair(n, pieces)
    sems += pair(2, n) + pair(2, n, 4) + pair(m, chunks) + pair(4)
    return buffers, sems


def fused_fits(n, m, seqs, tokens, width, inner):
    if m != 4 or n < 2 or tokens != LANES or inner < 4 * LANES:
        return False
    buffers, _ = fused_scratch(n, m, seqs, tokens, width, inner, 2 * LANES, 4 * LANES)
    size = 0
    for buffer in buffers:
        count = jnp.dtype(buffer.dtype).itemsize
        for extent in buffer.shape:
            count *= extent
        size += count
    return size + tokens * width * 2 < 48 * 2**20


def fused(n, m, states, gains, proj_a, proj_b, cotangent, src_len, tgt_len, dest):
    _, tokens, width = states.shape
    inner = proj_a.shape[2]
    buffers, sems = fused_scratch(n, m, src_len.shape[1], tokens, width, inner, 2 * LANES, 4 * LANES)
    bf16 = jnp.bfloat16
    grad = jax.ShapeDtypeStruct((n, tokens, inner), bf16)
    slices = jax.ShapeDtypeStruct((n, tokens, width // n), bf16)
    hbm = pl.BlockSpec(memory_space=pltpu.HBM)
    return pl.pallas_call(
        functools.partial(fused_kernel, n, m),
        out_shape=(jax.ShapeDtypeStruct((tokens, width), bf16), grad, grad, slices, slices),
        in_specs=[hbm] * 8,
        out_specs=[hbm] * 5,
        scratch_shapes=buffers + sems,
        compiler_params=pltpu.CompilerParams(
            collective_id=2, has_side_effects=True, vmem_limit_bytes=56 * 2**20
        ),
        name="fused",
    )(states, cotangent, gains, src_len, tgt_len, dest, proj_a, proj_b)


def grads_kernel(
    left_a, left_b, right_a, right_b, states_in, out_a, out_b, states_out,
    left, right, states, out, left_sem, right_sem, states_sem, out_sem,
):
    tiles, tile = out.shape[1:3]
    loads = []
    for which, (src_left, src_right) in enumerate(((left_a, right_a), (left_b, right_b))):
        loads.append((
            pltpu.make_async_copy(src_right, right.at[which], right_sem.at[which]),
            pltpu.make_async_copy(src_left, left.at[which], left_sem.at[which]),
        ))
    for pair in loads:
        for copy in pair:
            copy.start()
    bring = pltpu.make_async_copy(states_in, states, states_sem.at[0])
    give = pltpu.make_async_copy(states, states_out.at[0], states_sem.at[1])
    bring.start()

    def store(which, t):
        at = pl.ds(pl.multiple_of(t * tile, tile), tile)
        return pltpu.make_async_copy(
            out.at[which, t], (out_a, out_b)[which].at[0, at, :], out_sem.at[which, t]
        )

    for which in (0, 1):
        for copy in loads[which]:
            copy.wait()
        for t in range(tiles):
            part = left[which, :, t * tile : (t + 1) * tile]
            out[which, t] = left_product(part, right[which])
            store(which, t).start()
        if which == 0:
            bring.wait()
            give.start()
    for which in (0, 1):
        for t in range(tiles):
            store(which, t).wait()
    give.wait()


def grads(left_a, left_b, right_a, right_b, states):
    rows, cols = left_a.shape
    inner = right_a.shape[1]
    tokens, width = states.shape
    tile = min(cols, 2 * LANES)
    tiles = cols // tile
    bf16, f32 = jnp.bfloat16, jnp.float32
    dma = pltpu.SemaphoreType.DMA
    hbm = pl.BlockSpec(memory_space=pltpu.HBM)
    return pl.pallas_call(
        grads_kernel,
        out_shape=(
            jax.ShapeDtypeStruct((1, cols, inner), f32),
            jax.ShapeDtypeStruct((1, cols, inner), f32),
            jax.ShapeDtypeStruct((1, tokens, width), bf16),
        ),
        in_specs=[hbm] * 5,
        out_specs=[hbm] * 3,
        scratch_shapes=[
            pltpu.VMEM((2, rows, cols), bf16), pltpu.VMEM((2, rows, inner), bf16),
            pltpu.VMEM((tokens, width), bf16), pltpu.VMEM((2, tiles, tile, inner), f32),
            dma((2,)), dma((2,)), dma((2,)), dma((2, tiles)),
        ],
        compiler_params=pltpu.CompilerParams(vmem_limit_bytes=62 * 2**20),
        name="grads",
    )(left_a, left_b, right_a, right_b, states)


def per_device(states, gains, proj_a, proj_b, cotangent, src_len, tgt_len, dest):
    n = lax.axis_size("dp")
    m = lax.axis_size("mp")
    _, tokens, width = states.shape
    inner = proj_a.shape[2]
    args = (states, gains, proj_a, proj_b, cotangent, src_len, tgt_len, dest)
    if not fused_fits(n, m, src_len.shape[1], tokens, width, inner):
        return stepwise(*args)
    result, grad_first, grad_second, mine_a, mine_b = fused(n, m, *args)
    rows = n * tokens
    grad_a, grad_b, grad_states = grads(
        mine_a.reshape(rows, -1), mine_b.reshape(rows, -1),
        grad_first.reshape(rows, -1), grad_second.reshape(rows, -1), result,
    )
    return (grad_states, grad_a, grad_b)


def solution(mesh):
    return jax.shard_map(
        per_device,
        mesh=mesh,
        in_specs=(
            P("section", "dp", None),
            P("section", None),
            P("section", None, "mp"),
            P("section", None, "mp"),
            P("dp", None),
            P(),
            P(),
            P(),
        ),
        out_specs=(P("section", "dp", None), P("section", "dp", "mp"), P("section", "dp", "mp")),
        check_vma=False,
    )
```

```python
import functools

import jax
import jax.numpy as jnp
from jax import lax
from jax.experimental import pallas as pl
from jax.experimental.pallas import tpu as pltpu
from jax.sharding import PartitionSpec as P

HEAD_DIM = 64
LANES = 128
EPS = 1e-06
MAX_LEN = 16
MESH = pl.DeviceIdType.MESH


def rms_forward(states_row, gain):
    xf = states_row.astype(jnp.float32)
    scale = lax.rsqrt(jnp.mean(xf * xf, axis=-1, keepdims=True) + EPS)
    return (xf, scale, (xf * scale * gain).astype(jnp.bfloat16))


def left_product(left, right):
    return lax.dot_general(
        left, right, (((0,), (0,)), ((), ())), preferred_element_type=jnp.float32
    )


def right_product(rows, weight):
    return lax.dot_general(
        rows, weight, (((1,), (1,)), ((), ())), preferred_element_type=jnp.float32
    )


def sequence_of(lengths, names, tokens):
    slot = jnp.arange(lengths.shape[1], dtype=jnp.int32)
    before = slot[:, None] < slot[None, :]
    starts = jnp.sum(jnp.where(before[None], lengths[:, :, None], 0), axis=1)
    place = jnp.arange(tokens, dtype=jnp.int32)[None, :, None]
    offset = place - starts[:, None, :]
    inside = (offset >= 0) & (offset < lengths[:, None, :])
    return jnp.sum(jnp.where(inside, names[:, None, :], 0), axis=-1).reshape(-1)


def attend_piece(encoder, p, group, id_col, id_row, own, other, out_a, out_b, acc_a, acc_b):
    n, tokens, width = own.shape[1:]
    half = width // 2
    rows = n * tokens
    blocks = n // group
    lane = lax.broadcasted_iota(jnp.int32, (1, LANES), 1) // HEAD_DIM
    zero = jnp.zeros((), jnp.bfloat16)
    f32 = jnp.float32

    def cut(ref, which, c, at):
        lo = pl.multiple_of(which * half + c * LANES, LANES)
        return ref[p, at, :, pl.ds(lo, LANES)].reshape(-1, LANES)

    every = pl.ds(0, n)

    @pl.loop(0, half // LANES)
    def _(c):
        out_cols = pl.ds(pl.multiple_of(p * half + c * LANES, LANES), LANES)

        @pl.when(encoder)
        def _():
            keys, values = cut(own, 0, c, every), cut(own, 1, c, every)
            if blocks > 1:
                acc_a[...] = jnp.zeros_like(acc_a)
                acc_b[...] = jnp.zeros_like(acc_b)

            def block(b):
                at = pl.ds(b * group, group)
                query, dout = cut(other, 0, c, at), cut(other, 1, c, at)
                mask = id_col[...].reshape(rows, 1) == id_row[b]
                dk, dv = None, None
                for h in range(LANES // HEAD_DIM):
                    qh = jnp.where(lane == h, query, zero)
                    dh = jnp.where(lane == h, dout, zero)
                    expo = jnp.exp(jnp.where(mask, right_product(keys, qh), -jnp.inf))
                    weight = expo * (1.0 / jnp.sum(expo, axis=0, keepdims=True))
                    dweight = right_product(values, dh)
                    total = jnp.sum(weight * dweight, axis=0, keepdims=True)
                    dscore = (weight * (dweight - total)).astype(jnp.bfloat16)
                    pk = jnp.dot(dscore, qh, preferred_element_type=f32)
                    pv = jnp.dot(weight.astype(jnp.bfloat16), dh, preferred_element_type=f32)
                    dk = pk if dk is None else dk + pk
                    dv = pv if dv is None else dv + pv
                if blocks == 1:
                    out_a[:, :, out_cols] = dk.astype(jnp.bfloat16).reshape(n, tokens, LANES)
                    out_b[:, :, out_cols] = dv.astype(jnp.bfloat16).reshape(n, tokens, LANES)
                else:
                    acc_a[...] += dk
                    acc_b[...] += dv

            if blocks == 1:
                block(0)
            else:
                pl.loop(0, blocks)(block)
                out_a[:, :, out_cols] = acc_a[...].astype(jnp.bfloat16).reshape(n, tokens, LANES)
                out_b[:, :, out_cols] = acc_b[...].astype(jnp.bfloat16).reshape(n, tokens, LANES)

        @pl.when(jnp.logical_not(encoder))
        def _():
            keys, values = cut(other, 0, c, every), cut(other, 1, c, every)

            def block(b):
                at = pl.ds(b * group, group)
                query, dout = cut(own, 0, c, at), cut(own, 1, c, at)
                ids = id_col[at, :, :].reshape(group * tokens, 1)
                mask = None
                dq, att = None, None
                for h in range(LANES // HEAD_DIM):
                    kh = jnp.where(lane == h, keys, zero)
                    vh = jnp.where(lane == h, values, zero)
                    score = right_product(query, kh)
                    if mask is None:
                        span = group * tokens
                        mask = jnp.concatenate(
                            [ids == id_row[i] for i in range(rows // span)], axis=1
                        )
                    expo = jnp.exp(jnp.where(mask, score, -jnp.inf))
                    weight = expo * (1.0 / jnp.sum(expo, axis=1, keepdims=True))
                    dweight = right_product(dout, vh)
                    total = jnp.sum(weight * dweight, axis=1, keepdims=True)
                    dscore = (weight * (dweight - total)).astype(jnp.bfloat16)
                    pq = jnp.dot(dscore, kh, preferred_element_type=f32)
                    pa = jnp.dot(weight.astype(jnp.bfloat16), vh, preferred_element_type=f32)
                    dq = pq if dq is None else dq + pq
                    att = pa if att is None else att + pa
                shape = (group, tokens, LANES)
                out_a[at, :, out_cols] = dq.astype(jnp.bfloat16).reshape(shape)
                out_b[at, :, out_cols] = att.astype(jnp.bfloat16).reshape(shape)

            if blocks == 1:
                block(0)
            else:
                pl.loop(0, blocks)(block)


def forward_kernel(
    n, m, group, normed, second, id_col, id_row, proj_a, proj_b,
    out_a, out_b, mine_a, mine_b,
    wbuf, paired, own, other, acc_a, acc_b, wsem,
    line_send, line_recv, sec_send, sec_recv, za_send, za_recv, mp_send, mp_recv, loc_sem,
):
    me = lax.axis_index("dp")
    col = lax.axis_index("mp")
    sec = lax.axis_index("section")
    tokens, width = normed.shape
    pieces = wbuf.shape[1]
    half = wbuf.shape[3]
    part = tokens // m
    cols = width // n

    def weight_copy(which, p):
        src = (proj_a, proj_b)[which]
        return pltpu.make_async_copy(
            src.at[0, :, pl.ds(p * half, half)], wbuf.at[which, p], wsem.at[which, p]
        )

    for p in range(pieces):
        for which in (0, 1):
            weight_copy(which, p).start()

    barrier = pltpu.get_barrier_semaphore()
    for j in range(1, n):
        pl.semaphore_signal(
            barrier, inc=1, device_id={"dp": lax.rem(me + j, n)}, device_id_type=MESH
        )
    for j in range(1, m):
        pl.semaphore_signal(
            barrier, inc=1, device_id={"mp": lax.rem(col + j, m)}, device_id_type=MESH
        )
    pl.semaphore_signal(barrier, inc=1, device_id={"section": 1 - sec}, device_id_type=MESH)
    pl.semaphore_wait(barrier, n + m - 1)

    band = pl.ds(pl.multiple_of(col * part, part), part)

    def line_copy(way, s, p):
        chunk = me - s if way == 0 else me + s
        target = me + 1 if way == 0 else me - 1
        src = paired.at[p] if s == 0 else own.at[p, chunk]
        return pltpu.make_async_remote_copy(
            src_ref=src, dst_ref=own.at[p, chunk],
            send_sem=line_send.at[way, s, p], recv_sem=line_recv.at[way, s, p],
            device_id={"dp": target}, device_id_type=MESH,
        )

    def line_ok(way, s):
        if way == 0:
            return jnp.logical_and(me - s >= 0, me < n - 1)
        return jnp.logical_and(me + s <= n - 1, me > 0)

    def got(way, s):
        return me - 1 - s >= 0 if way == 0 else me + 1 + s <= n - 1

    def sec_copy(chunk, p, src):
        return pltpu.make_async_remote_copy(
            src_ref=src, dst_ref=other.at[p, chunk],
            send_sem=sec_send.at[chunk, p], recv_sem=sec_recv.at[chunk, p],
            device_id={"section": 1 - sec}, device_id_type=MESH,
        )

    def za_copy(which, j):
        src, dst = ((normed, mine_a), (second, mine_b))[which]
        peer = lax.rem(me + j, n)
        return pltpu.make_async_remote_copy(
            src_ref=src.at[band, pl.ds(pl.multiple_of(peer * cols, cols), cols)],
            dst_ref=dst.at[me, band, :],
            send_sem=za_send.at[which, j], recv_sem=za_recv.at[which, j],
            device_id={"dp": peer}, device_id_type=MESH,
        )

    def mp_copy(which, j):
        dst = (mine_a, mine_b)[which]
        return pltpu.make_async_remote_copy(
            src_ref=dst.at[:, band, :], dst_ref=dst.at[:, band, :],
            send_sem=mp_send.at[which, j], recv_sem=mp_recv.at[which, j],
            device_id={"mp": lax.rem(col + j, m)}, device_id_type=MESH,
        )

    def local(which):
        src, dst = ((normed, mine_a), (second, mine_b))[which]
        return pltpu.make_async_copy(
            src.at[band, pl.ds(pl.multiple_of(me * cols, cols), cols)],
            dst.at[me, band, :], loc_sem.at[which],
        )

    def keep(p):
        return pltpu.make_async_copy(paired.at[p], own.at[p, me], loc_sem.at[2 + p])

    def second_too(fn):
        fn(0)
        pl.when(sec == 1)(lambda: fn(1))

    for j in range(1, n):
        second_too(lambda which: za_copy(which, j).start())
    second_too(lambda which: local(which).start())

    for p in range(pieces):
        for which in (0, 1):
            weight_copy(which, p).wait()
            rows_in = (normed, second)[which]
            paired[p, :, which * half : (which + 1) * half] = jnp.dot(
                rows_in[...], wbuf[which, p], preferred_element_type=jnp.float32
            ).astype(jnp.bfloat16)
        for way in (0, 1):
            pl.when(line_ok(way, 0))(lambda way=way, p=p: line_copy(way, 0, p).start())
        sec_copy(me, p, paired.at[p]).start()
        keep(p).start()

    def spread(which):
        local(which).wait()
        for j in range(1, n):
            za_copy(which, j).wait_recv()
        for j in range(1, m):
            mp_copy(which, j).start()

    second_too(spread)

    for wave in range(pieces + n - 2):
        for s in range(max(0, wave - pieces + 1), min(n - 1, wave + 1)):
            p = wave - s
            for way in (0, 1):

                @pl.when(got(way, s))
                def _():
                    line_copy(way, s, p).wait_recv()
                    chunk = me - 1 - s if way == 0 else me + 1 + s
                    if s + 1 < n - 1:
                        pl.when(line_ok(way, s + 1))(
                            lambda: line_copy(way, s + 1, p).start()
                        )
                    sec_copy(chunk, p, own.at[p, chunk]).start()

        p = wave - (n - 2)
        if p >= 0:
            keep(p).wait()
            for c in range(n):
                sec_copy(c, p, own.at[p, c]).wait_recv()
            attend_piece(
                sec == 0, p, group, id_col, id_row, own, other, out_a, out_b, acc_a, acc_b
            )

    def finish(which):
        for j in range(1, n):
            za_copy(which, j).wait_send()
        for j in range(1, m):
            mp_copy(which, j).wait()

    second_too(finish)
    for p in range(pieces):
        for s in range(n - 1):
            for way in (0, 1):
                pl.when(line_ok(way, s))(
                    lambda way=way, s=s, p=p: line_copy(way, s, p).wait_send()
                )
        for c in range(n):
            sec_copy(c, p, own.at[p, c]).wait_send()


def forward(n, m, normed, second, id_c, id_r, proj_a, proj_b):
    tokens, width = normed.shape
    inner = proj_a.shape[2]
    half = 2 * LANES
    pieces = inner // half
    rows = n * tokens
    group = max(1, min(n, 512 * 512 // (rows * tokens)))
    blocks = n // group
    grad = jax.ShapeDtypeStruct((n, tokens, inner), jnp.bfloat16)
    mine = jax.ShapeDtypeStruct((n, tokens, width // n), jnp.bfloat16)
    acc = (rows, LANES) if blocks > 1 else (8, LANES)
    dma = pltpu.SemaphoreType.DMA
    vmem = pl.BlockSpec(memory_space=pltpu.VMEM)
    anyw = pl.BlockSpec(memory_space=pltpu.HBM)
    bf16 = jnp.bfloat16
    return pl.pallas_call(
        functools.partial(forward_kernel, n, m, group),
        out_shape=(grad, grad, mine, mine),
        in_specs=[vmem] * 4 + [anyw] * 2,
        out_specs=[vmem, vmem, anyw, anyw],
        scratch_shapes=[
            pltpu.VMEM((2, pieces, width, half), bf16),
            pltpu.VMEM((pieces, tokens, 2 * half), bf16),
            pltpu.VMEM((pieces, n, tokens, 2 * half), bf16),
            pltpu.VMEM((pieces, n, tokens, 2 * half), bf16),
            pltpu.VMEM(acc, jnp.float32), pltpu.VMEM(acc, jnp.float32),
            dma((2, pieces)),
            dma((2, n, pieces)), dma((2, n, pieces)), dma((n, pieces)), dma((n, pieces)),
            dma((2, n)), dma((2, n)), dma((2, m)), dma((2, m)), dma((2 + pieces,)),
        ],
        compiler_params=pltpu.CompilerParams(
            collective_id=0, has_side_effects=True, vmem_limit_bytes=67000000
        ),
        name="forward",
    )(normed, second, id_c.reshape(n, tokens, 1), id_r.reshape(blocks, 1, rows // blocks),
      proj_a, proj_b)


def reduce_kernel(
    m, grad_a, grad_b, proj_a, proj_b, x_ref, gain_ref, result,
    left, wbuf, total, mine, partial, landed, gsem, wsem, send, recv,
):
    me = lax.axis_index("dp")
    col = lax.axis_index("mp")
    encoder = lax.axis_index("section") == 0
    tokens = x_ref.shape[0]
    part = tokens // m
    chunks, step = wbuf.shape[1:3]

    def left_copy(which):
        return pltpu.make_async_copy(
            (grad_a, grad_b)[which].at[me], left.at[which], gsem.at[which]
        )

    def weight_copy(which, c):
        return pltpu.make_async_copy(
            (proj_a, proj_b)[which].at[0, pl.ds(c * step, step), :],
            wbuf.at[which, c], wsem.at[which, c],
        )

    left_copy(0).start()
    pl.when(encoder)(lambda: left_copy(1).start())
    for c in range(chunks):
        weight_copy(0, c).start()
        pl.when(encoder)(lambda c=c: weight_copy(1, c).start())

    barrier = pltpu.get_barrier_semaphore()
    for j in range(1, m):
        pl.semaphore_signal(
            barrier, inc=1, device_id={"mp": lax.rem(col + j, m)}, device_id_type=MESH
        )
    pl.semaphore_wait(barrier, m - 1)

    def scatter(j, c):
        peer = lax.rem(col + j, m)
        rows = pl.ds(pl.multiple_of(peer * part, part), part)
        at = pl.ds(c * step, step)
        return pltpu.make_async_remote_copy(
            src_ref=partial.at[rows, at], dst_ref=landed.at[j, :, at],
            send_sem=send.at[j, c], recv_sem=recv.at[j, c],
            device_id={"mp": peer}, device_id_type=MESH,
        )

    band = pl.ds(pl.multiple_of(col * part, part), part)
    left_copy(0).wait()
    pl.when(encoder)(lambda: left_copy(1).wait())
    for c in range(chunks):
        weight_copy(0, c).wait()
        total[...] = right_product(left[0], wbuf[0, c])

        @pl.when(encoder)
        def _():
            weight_copy(1, c).wait()
            total[...] += right_product(left[1], wbuf[1, c])

        partial[:, c * step : (c + 1) * step] = total[...].astype(jnp.bfloat16)
        mine[:, c * step : (c + 1) * step] = total[band, :]
        for j in range(1, m):
            scatter(j, c).start()
    x = x_ref[band, :].astype(jnp.float32)
    scale = lax.rsqrt(jnp.mean(x * x, axis=-1, keepdims=True) + EPS)
    for j in range(1, m):
        for c in range(chunks):
            scatter(j, c).wait_recv()
    dnorm = mine[...]
    for j in range(1, m):
        dnorm = dnorm + landed[j].astype(jnp.float32)
    upper = gain_ref[...] * dnorm
    inner = jnp.mean(x * upper, axis=-1, keepdims=True)
    result[...] = (scale * upper - x * scale * scale * scale * inner).astype(jnp.bfloat16)
    for j in range(1, m):
        for c in range(chunks):
            scatter(j, c).wait_send()


def reduce_norm(m, grad_a, grad_b, proj_a, proj_b, states, gain):
    tokens, width = states.shape
    inner = proj_a.shape[2]
    part = tokens // m
    step = 4 * LANES
    chunks = width // step
    dma = pltpu.SemaphoreType.DMA
    bf16, f32 = jnp.bfloat16, jnp.float32
    vmem = pl.BlockSpec(memory_space=pltpu.VMEM)
    return pl.pallas_call(
        functools.partial(reduce_kernel, m),
        out_shape=jax.ShapeDtypeStruct((part, width), bf16),
        in_specs=[pl.BlockSpec(memory_space=pltpu.HBM)] * 4 + [vmem] * 2,
        out_specs=vmem,
        scratch_shapes=[
            pltpu.VMEM((2, tokens, inner), bf16),
            pltpu.VMEM((2, chunks, step, inner), bf16),
            pltpu.VMEM((tokens, step), f32),
            pltpu.VMEM((part, width), f32),
            pltpu.VMEM((tokens, width), bf16),
            pltpu.VMEM((m, part, width), bf16),
            dma((2,)), dma((2, chunks)), dma((m, chunks)), dma((m, chunks)),
        ],
        compiler_params=pltpu.CompilerParams(
            collective_id=1, has_side_effects=True, vmem_limit_bytes=66500000
        ),
        name="reduce_norm",
    )(grad_a, grad_b, proj_a, proj_b, states, gain)


def stepwise(states, gains, proj_a, proj_b, cotangent, src_len, tgt_len, dest):
    encoder = lax.axis_index("section") == 0
    member = lax.axis_index("dp")
    n = lax.axis_size("dp")
    m = lax.axis_size("mp")
    gain = gains[0]
    weight_a = proj_a[0]
    weight_b = proj_b[0]
    tokens = states.shape[1]
    _, _, normed = rms_forward(states[0], gain)
    second_left = jnp.where(encoder, normed, cotangent)
    rows = n * tokens
    seqs = tgt_len.shape[1]
    names = jnp.arange(n * seqs, dtype=jnp.int32).reshape(n, seqs)
    id_c = sequence_of(
        jnp.where(encoder, src_len, tgt_len), jnp.where(encoder, dest, names), tokens
    )
    id_r = sequence_of(
        jnp.where(encoder, tgt_len, src_len), jnp.where(encoder, names, dest), tokens
    )
    grad_first, grad_second, mine_a, mine_b = forward(
        n, m, normed, second_left, id_c, id_r, proj_a, proj_b
    )
    mine = reduce_norm(m, grad_first, grad_second, proj_a, proj_b, states[0], gains)
    col = lax.axis_index("mp")
    landed = [mine] + [
        lax.ppermute(mine, "mp", [(i, (i + j) % m) for i in range(m)]) for j in range(1, m)
    ]
    mine_a = mine_a.reshape(rows, -1)
    mine_b = jnp.where(encoder, mine_a, mine_b.reshape(rows, -1))
    grad_a = left_product(mine_a, grad_first.reshape(rows, -1))
    grad_b = left_product(mine_b, grad_second.reshape(rows, -1))
    bands = []
    for b in range(m):
        band = landed[0]
        for j in range(1, m):
            band = jnp.where(col == (b + j) % m, landed[j], band)
        bands.append(band)
    grad_states = jnp.concatenate(bands, axis=0)
    return (grad_states[None], grad_a[None], grad_b[None])


def packed_ids(lengths, names, tokens):
    n, seqs = lengths.shape
    place = lax.broadcasted_iota(jnp.int32, (n, tokens), 1)
    start = jnp.zeros((n, 1), jnp.int32)
    ids = jnp.zeros((n, tokens), jnp.int32)
    for i in range(seqs):
        length = lengths[:, i : i + 1]
        offset = place - start
        ids = jnp.where((offset >= 0) & (offset < length), names(i), ids)
        start = start + length
    return (ids + 1).astype(jnp.float32)


def fused_kernel(
    n, m, x_hbm, cot_hbm, gain_hbm, src_hbm, tgt_hbm, dest_hbm, proj_a, proj_b,
    result, out_a, out_b, mine_a, mine_b,
    gain, src_len, tgt_len, dest, rest, x, xall, wbuf, own, other, grad_a, grad_b, id_col, id_row, pick, id_far, far, total, partial, landed,
    gate, in_sem, wsem, loc_sem, out_sem, zx_send, zx_recv, px_send, px_recv, line_send, line_recv,
    sec_send, sec_recv, za_send, za_recv, sl_send, sl_recv, rs_send, rs_recv, ag_send, ag_recv,
):
    me = lax.axis_index("dp")
    col = lax.axis_index("mp")
    sec = lax.axis_index("section")
    encoder = sec == 0
    decoder = sec == 1
    tokens, width = x.shape
    pieces, half = wbuf.shape[1], wbuf.shape[3]
    part = tokens // m
    cols = width // n
    rows = n * tokens
    chunks = rs_send.shape[1]
    step = width // chunks
    quarter = width // pieces
    hops = (n - 1) * pieces
    seqs = src_len.shape[1]
    cap = far.shape[0]
    f32, bf16 = jnp.float32, jnp.bfloat16
    spare = lax.rem(me + 1, n)
    near_x = col + 1 - 2 * lax.rem(col, 2)
    near_y = lax.rem(col + 2, m)
    band = pl.ds(pl.multiple_of(col * part, part), part)
    lane = lax.broadcasted_iota(jnp.int32, (1, LANES), 1) // HEAD_DIM
    zero = jnp.zeros((), bf16)

    def remote(src, dst, send, recv, **device):
        return pltpu.make_async_remote_copy(
            src_ref=src, dst_ref=dst, send_sem=send, recv_sem=recv,
            device_id=device, device_id_type=MESH,
        )

    def weight_copy(which, p):
        src = (proj_a, proj_b)[which]
        return pltpu.make_async_copy(
            src.at[0, :, pl.ds(pl.multiple_of(p * half, half), half)],
            wbuf.at[which, p], wsem.at[which, p],
        )

    x_copy = pltpu.make_async_copy(x_hbm.at[0], x, in_sem.at[0])
    cot_copy = pltpu.make_async_copy(cot_hbm, xall.at[spare], in_sem.at[1])
    small_copies = [
        pltpu.make_async_copy(src, dst, in_sem.at[2 + i])
        for i, (src, dst) in enumerate(
            ((gain_hbm, gain), (src_hbm, src_len), (tgt_hbm, tgt_len), (dest_hbm, dest))
        )
    ]
    x_copy.start()
    for copy in small_copies:
        copy.start()
    pl.when(decoder)(cot_copy.start)
    for p in range(pieces):
        for which in (0, 1):
            weight_copy(which, p).start()

    barrier = pltpu.get_barrier_semaphore()
    for j in range(1, n):
        pl.semaphore_signal(
            barrier, inc=1, device_id={"dp": lax.rem(me + j, n)}, device_id_type=MESH
        )
    for j in range(1, m):
        pl.semaphore_signal(
            barrier, inc=1, device_id={"mp": lax.rem(col + j, m)}, device_id_type=MESH
        )
    pl.semaphore_signal(barrier, inc=1, device_id={"section": 1 - sec}, device_id_type=MESH)
    x_copy.wait()
    for copy in small_copies:
        copy.wait()
    group = min(tokens, 16)

    @pl.loop(0, tokens // group)
    def _(r):
        at = pl.ds(pl.multiple_of(r * group, group), group)
        xf = x[at, :].astype(f32)
        scale = lax.rsqrt(jnp.mean(xf * xf, axis=-1, keepdims=True) + EPS)
        xall[me, at, :] = (xf * scale * gain[...]).astype(bf16)

    pl.semaphore_wait(barrier, n + m - 1)

    def source(way, s):
        return me - (1 - 2 * way) * (1 + s)

    def got(way, s):
        src = source(way, s)
        return jnp.logical_and(src >= 0, src < n)

    def line_ok(way, s):
        chunk = source(way, s - 1)
        target = me + 1 - 2 * way
        inside = jnp.logical_and(chunk >= 0, chunk < n)
        return jnp.logical_and(inside, jnp.logical_and(target >= 0, target < n))

    def span(q):
        return pl.ds(pl.multiple_of(q * quarter, quarter), quarter)

    def zx_copy(way, s, q):
        ref = xall.at[source(way, s - 1), band, span(q)]
        return remote(
            ref, ref, zx_send.at[way, s, q], zx_recv.at[way, s, q], dp=me + 1 - 2 * way
        )

    def line_copy(way, s, p):
        ref = own.at[p, source(way, s - 1)]
        return remote(
            ref, ref, line_send.at[way, s, p], line_recv.at[way, s, p], dp=me + 1 - 2 * way
        )

    def sec_copy(chunk, p):
        return remote(
            own.at[p, chunk], other.at[p, chunk],
            sec_send.at[chunk, p], sec_recv.at[chunk, p], section=1 - sec,
        )

    def plane(view, send, recv, kind):
        small = part // 2
        start = (col * part, col * part, near_x * part, near_y * part + small)[kind]
        size = (part, part, small, small)[kind]
        target = (near_x, near_y, near_y, near_x)[kind]
        ref = view(pl.ds(pl.multiple_of(start, small), size))
        return remote(ref, ref, send.at[kind], recv.at[kind], mp=target)

    def px_copy(src, q, kind):
        return plane(
            lambda at: xall.at[src, at, span(q)], px_send.at[src, q], px_recv.at[src, q], kind
        )

    def za_copy(which, j):
        peer = lax.rem(me + j, n)
        src = xall.at[(me, spare)[which]]
        return remote(
            src.at[band, pl.ds(pl.multiple_of(peer * cols, cols), cols)],
            (mine_a, mine_b)[which].at[me, band, :],
            za_send.at[which, j], za_recv.at[which, j], dp=peer,
        )

    def sl_copy(which, j, kind):
        block = lax.rem(me + n - j, n)
        return plane(
            lambda at: (mine_a, mine_b)[which].at[block, at, :],
            sl_send.at[which, j], sl_recv.at[which, j], kind,
        )

    def scatter(j, d):
        peer = lax.rem(col + j, m)
        at = pl.ds(pl.multiple_of(d * step, step), step)
        return remote(
            partial.at[pl.ds(pl.multiple_of(peer * part, part), part), at],
            landed.at[j, :, at], rs_send.at[j, d], rs_recv.at[j, d], mp=peer,
        )

    def gather(kind):
        if kind > 1:
            return plane(lambda at: result.at[at, :], ag_send, ag_recv, kind)
        return remote(
            rest, result.at[band, :], ag_send.at[kind], ag_recv.at[kind],
            mp=(near_x, near_y)[kind],
        )

    keep_rest = pltpu.make_async_copy(rest, result.at[band, :], loc_sem.at[2])

    my_cols = pl.ds(pl.multiple_of(me * cols, cols), cols)

    def keep_slice(which):
        src = xall.at[(me, spare)[which]]
        return pltpu.make_async_copy(
            src.at[:, my_cols], (mine_a, mine_b)[which].at[me], loc_sem.at[which]
        )

    def keep_all(which):
        return pltpu.make_async_copy(
            xall.at[:, :, my_cols], (mine_a, mine_b)[which], loc_sem.at[which]
        )

    def grad_out(which, p):
        of = pl.ds(pl.multiple_of(p * half, half), half)
        return pltpu.make_async_copy(
            (grad_a, grad_b)[which].at[:, :, of], (out_a, out_b)[which].at[:, :, of],
            out_sem.at[which, p],
        )

    @pl.when(decoder)
    def _():
        cot_copy.wait()
        for j in range(1, n):
            za_copy(1, j).start()

    @pl.when(encoder)
    def _():
        for q in range(pieces):
            for way in (0, 1):
                pl.when(line_ok(way, 0))(lambda way=way, q=q: zx_copy(way, 0, q).start())

    @pl.when(decoder)
    def _():
        for j in range(1, n):
            za_copy(0, j).start()
        for which in (0, 1):
            keep_slice(which).start()

    src_ids = packed_ids(src_len, lambda i: dest[:, i : i + 1], tokens)
    device = lax.broadcasted_iota(jnp.int32, (n, 1), 0)
    tgt_ids = packed_ids(tgt_len, lambda i: device * seqs + i, tokens)
    id_row[...] = jnp.where(encoder, tgt_ids, src_ids)
    near_ids = jnp.where(encoder, src_ids, tgt_ids)
    for b in range(n):
        id_col[b] = jnp.transpose(jnp.broadcast_to(near_ids[b : b + 1, :], (LANES, tokens)))
    flat = jnp.concatenate([id_row[b : b + 1, :] for b in range(n)], axis=1)
    flat = jnp.broadcast_to(flat, (16, rows)).astype(bf16)
    before = lax.broadcasted_iota(jnp.int32, (rows, rows), 0)
    before = before < lax.broadcasted_iota(jnp.int32, (rows, rows), 1)
    before = jnp.where(before, 1.0, 0.0).astype(bf16)
    slot = lax.broadcasted_iota(jnp.int32, (cap, rows), 0).astype(f32)
    for b in range(n):
        member = jnp.concatenate(
            [
                jnp.max(
                    jnp.where(id_col[b] == id_row[c : c + 1, :], 1.0, 0.0), axis=0, keepdims=True
                )
                for c in range(n)
            ],
            axis=1,
        )
        rank = jnp.dot(
            jnp.broadcast_to(member, (16, rows)).astype(bf16), before, preferred_element_type=f32
        )[0:1, :]
        key = jnp.where(member > 0.0, rank, -1.0)
        chosen = jnp.where(key == slot, 1.0, 0.0).astype(bf16)
        pick[b] = chosen
        id_far[b] = right_product(flat, chosen)

    def project(p, blk_a, blk_b, out):
        for which in (0, 1):
            own[p, out, :, which * half : (which + 1) * half] = jnp.dot(
                xall[(blk_a, blk_b)[which]], wbuf[which, p], preferred_element_type=f32
            ).astype(bf16)
        sec_copy(out, p).start()

    def x_line(i):
        s, q = i // pieces, i % pieces
        for way in (0, 1):

            @pl.when(got(way, s))
            def _():
                zx_copy(way, s, q).wait_recv()
                pl.when(line_ok(way, s + 1))(lambda: zx_copy(way, s + 1, q).start())
                for kind in (0, 1):
                    px_copy(source(way, s), q, kind).start()

    def x_near(i):
        s, q = i // pieces, i % pieces
        for way in (0, 1):

            @pl.when(got(way, s))
            def _():
                for kind in (0, 1):
                    px_copy(source(way, s), q, kind).wait_recv()
                    px_copy(source(way, s), q, 2 + kind).start()

    def x_done(i):
        s, q = i // pieces, i % pieces
        for way in (0, 1):

            @pl.when(got(way, s))
            def _():
                for kind in (2, 3):
                    px_copy(source(way, s), q, kind).wait_recv()

    def x_work(i):
        @pl.loop(0, 2)
        def _(way):
            src = source(way, i // pieces)
            pl.when(got(way, i // pieces))(lambda: project(i % pieces, src, src, src))

    @pl.loop(0, pieces)
    def _(p):
        for which in (0, 1):
            weight_copy(which, p).wait()
        project(p, me, lax.rem(me + sec, n), me)

    heads = LANES // HEAD_DIM

    def stack(near):
        return jnp.concatenate([jnp.where(lane == h, near, zero) for h in range(heads)], axis=0)

    def merge(left, right):
        whole = jnp.dot(left.reshape(-1, cap), right, preferred_element_type=f32)
        whole = whole.reshape(heads, tokens, LANES)
        picked = whole[0]
        for h in range(1, heads):
            picked = jnp.where(lane == h, whole[h], picked)
        return picked.astype(bf16)

    def unit(axis, p, blk):
        far[...] = jnp.dot(
            pick[blk], other[p].reshape(rows, 2 * half), preferred_element_type=f32
        ).astype(bf16)
        mask = jnp.concatenate(
            [
                id_col[blk] == id_far[blk, 0:1, c * LANES : (c + 1) * LANES]
                for c in range(cap // LANES)
            ],
            axis=1,
        )

        @pl.loop(0, half // LANES, unroll=True)
        def _(c):
            lo = pl.ds(pl.multiple_of(c * LANES, LANES), LANES)
            hi = pl.ds(pl.multiple_of(half + c * LANES, LANES), LANES)
            at = pl.ds(pl.multiple_of(p * half + c * LANES, LANES), LANES)
            near_a, near_b = own[p, blk, :, lo], own[p, blk, :, hi]
            far_a, far_b = far[:, lo], far[:, hi]
            score = right_product(stack(near_a), far_a).reshape(heads, tokens, cap)
            expo = jnp.exp(jnp.where(mask[None], score, -jnp.inf))
            norm = jnp.sum(expo, axis=axis + 1, keepdims=True)
            weight = expo * (1.0 / jnp.where(norm == 0.0, 1.0, norm))
            dweight = right_product(stack(near_b), far_b).reshape(heads, tokens, cap)
            shift = jnp.sum(weight * dweight, axis=axis + 1, keepdims=True)
            dscore = (weight * (dweight - shift)).astype(bf16)
            grad_a[blk, :, at] = merge(dscore, far_a)
            grad_b[blk, :, at] = merge(weight.astype(bf16), far_b)

    def others(axis, p):
        @pl.loop(1, n)
        def _(j):
            unit(axis, p, lax.rem(me + j, n))

    def ready(p):
        for c in range(n):
            sec_copy(c, p).wait_recv()

    def reduce_own(which_all):
        @pl.loop(0, chunks, unroll=2)
        def _(d):
            at = pl.ds(pl.multiple_of(d * step, step), step)
            acc = None
            for which in which_all:
                for p in range(pieces):
                    left = (grad_a, grad_b)[which][me, :, p * half : (p + 1) * half]
                    term = right_product(left, wbuf[which, p, at, :])
                    acc = term if acc is None else acc + term
            total[:, at] = acc
            partial[:, at] = acc.astype(bf16)
            for j in range(1, m):
                scatter(j, d).start()

    def finish_own():
        xf = x[band, :].astype(f32)
        scale = lax.rsqrt(jnp.mean(xf * xf, axis=-1, keepdims=True) + EPS)
        for j in range(1, m):
            for d in range(chunks):
                scatter(j, d).wait_recv()
        dnorm = total[band, :]
        for j in range(1, m):
            dnorm = dnorm + landed[j].astype(f32)
        upper = gain[...] * dnorm
        inner = jnp.mean(xf * upper, axis=-1, keepdims=True)
        rest[...] = (scale * upper - xf * scale * scale * scale * inner).astype(bf16)
        gather(0).start()
        gather(1).start()
        keep_rest.start()

    def relay_own():
        for kind in (0, 1):
            gather(kind).wait_recv()
            gather(2 + kind).start()

    def wave(w):
        for s in range(max(0, w - pieces + 1), min(n - 1, w + 1)):
            p = w - s
            for way in (0, 1):

                @pl.when(got(way, s))
                def _():
                    line_copy(way, s, p).wait_recv()
                    if s + 1 < n - 1:
                        pl.when(line_ok(way, s + 1))(
                            lambda: line_copy(way, s + 1, p).start()
                        )
                    sec_copy(source(way, s), p).start()

    @pl.when(encoder)
    def _():
        lags = (0, 2, 5, 4 + pieces)

        @pl.loop(0, hops + lags[3])
        def _(i):
            for lag, stage in zip(lags, (x_line, x_near, x_done, x_work)):
                at = i - lag
                inside = jnp.logical_and(at >= 0, at < hops)
                pl.when(inside)(lambda stage=stage, at=at: stage(at))

            @pl.when(i == 1)
            def _():
                pl.semaphore_signal(
                    gate, inc=1, device_id={"section": 1 - sec}, device_id_type=MESH
                )

        for which in (0, 1):
            keep_all(which).start()

        @pl.loop(0, pieces)
        def _(p):
            ready(p)
            unit(0, p, me)

        reduce_own((0, 1))

        @pl.loop(0, pieces)
        def _(p):
            others(0, p)
            for which in (0, 1):
                grad_out(which, p).start()
            pl.when(p == 1)(finish_own)
            pl.when(p == 2)(relay_own)


        @pl.loop(0, hops)
        def _(i):
            s, q = i // pieces, i % pieces
            for way in (0, 1):
                pl.when(line_ok(way, s))(lambda way=way: zx_copy(way, s, q).wait_send())

                @pl.when(got(way, s))
                def _():
                    for kind in range(4):
                        px_copy(source(way, s), q, kind).wait_send()

        for which in (0, 1):
            keep_all(which).wait()

    @pl.when(decoder)
    def _():
        pl.semaphore_wait(gate, 1)
        for p in range(pieces):
            for way in (0, 1):
                pl.when(line_ok(way, 0))(
                    lambda way=way, p=p: line_copy(way, 0, p).start()
                )
        for w in range(pieces):
            wave(w)
        for which in (0, 1):
            for j in range(1, n):
                za_copy(which, j).wait_recv()
                for kind in (0, 1):
                    sl_copy(which, j, kind).start()

        @pl.loop(0, pieces)
        def _(p):
            ready(p)
            unit(1, p, me)
            for late in range(n - 2):
                pl.when(p == min(late, pieces - 1))(lambda late=late: wave(pieces + late))

        reduce_own((0,))
        for which in (0, 1):
            for j in range(1, n):
                for kind in (0, 1):
                    sl_copy(which, j, kind).wait_recv()
                    sl_copy(which, j, 2 + kind).start()
        @pl.loop(0, pieces)
        def _(p):
            others(1, p)
            for which in (0, 1):
                grad_out(which, p).start()
            pl.when(p == 1)(finish_own)
            pl.when(p == 2)(relay_own)

        for which in (0, 1):
            keep_slice(which).wait()
            for j in range(1, n):
                za_copy(which, j).wait_send()
                for kind in range(4):
                    sl_copy(which, j, kind).wait_send()
                for kind in (2, 3):
                    sl_copy(which, j, kind).wait_recv()
        for p in range(pieces):
            for s in range(n - 1):
                for way in (0, 1):
                    pl.when(line_ok(way, s))(
                        lambda way=way, s=s, p=p: line_copy(way, s, p).wait_send()
                    )

    for p in range(pieces):
        for c in range(n):
            sec_copy(c, p).wait_send()
    for j in range(1, m):
        for d in range(chunks):
            scatter(j, d).wait_send()
    for kind in range(4):
        gather(kind).wait_send()
    for kind in (2, 3):
        gather(kind).wait_recv()
    keep_rest.wait()
    for which in (0, 1):
        for p in range(pieces):
            grad_out(which, p).wait()


def fused_scratch(n, m, seqs, tokens, width, inner, half, step):
    pieces = inner // half
    part = tokens // m
    cap = min(n * tokens, seqs * MAX_LEN)
    chunks = width // step
    dma = pltpu.SemaphoreType.DMA
    vmem = pltpu.VMEM
    bf16, f32 = jnp.bfloat16, jnp.float32
    buffers = [
        vmem((1, width), f32), vmem((n, seqs), jnp.int32), vmem((n, seqs), jnp.int32),
        vmem((n, seqs), jnp.int32), vmem((part, width), bf16),
        vmem((tokens, width), bf16), vmem((n, tokens, width), bf16),
        vmem((2, pieces, width, half), bf16),
        vmem((pieces, n, tokens, 2 * half), bf16), vmem((pieces, n, tokens, 2 * half), bf16),
        vmem((n, tokens, inner), bf16), vmem((n, tokens, inner), bf16),
        vmem((n, tokens, LANES), f32), vmem((n, tokens), f32),
        vmem((n, cap, n * tokens), bf16), vmem((n, 16, cap), f32), vmem((cap, 2 * half), bf16),
        vmem((tokens, width), f32), vmem((tokens, width), bf16), vmem((m, part, width), bf16),
    ]
    pair = lambda *shape: [dma(shape), dma(shape)]
    sems = [pltpu.SemaphoreType.REGULAR, dma((6,)), dma((2, pieces)), dma((3,)), dma((2, pieces))]
    sems += pair(2, n, pieces) + pair(n, pieces, 4) + pair(2, n, pieces) + pair(n, pieces)
    sems += pair(2, n) + pair(2, n, 4) + pair(m, chunks) + pair(4)
    return buffers, sems


def fused_fits(n, m, seqs, tokens, width, inner):
    if m != 4 or n < 2 or tokens != LANES or inner < 4 * LANES or n * seqs > 256:
        return False
    buffers, _ = fused_scratch(n, m, seqs, tokens, width, inner, 2 * LANES, 4 * LANES)
    size = 0
    for buffer in buffers:
        count = jnp.dtype(buffer.dtype).itemsize
        for extent in buffer.shape:
            count *= extent
        size += count
    return size + tokens * width * 2 < 48 * 2**20


def fused(n, m, states, gains, proj_a, proj_b, cotangent, src_len, tgt_len, dest):
    _, tokens, width = states.shape
    inner = proj_a.shape[2]
    buffers, sems = fused_scratch(n, m, src_len.shape[1], tokens, width, inner, 2 * LANES, 4 * LANES)
    bf16 = jnp.bfloat16
    grad = jax.ShapeDtypeStruct((n, tokens, inner), bf16)
    slices = jax.ShapeDtypeStruct((n, tokens, width // n), bf16)
    hbm = pl.BlockSpec(memory_space=pltpu.HBM)
    return pl.pallas_call(
        functools.partial(fused_kernel, n, m),
        out_shape=(jax.ShapeDtypeStruct((tokens, width), bf16), grad, grad, slices, slices),
        in_specs=[hbm] * 8,
        out_specs=[hbm] * 5,
        scratch_shapes=buffers + sems,
        compiler_params=pltpu.CompilerParams(
            collective_id=2, has_side_effects=True, vmem_limit_bytes=56 * 2**20
        ),
        name="fused",
    )(states, cotangent, gains, src_len, tgt_len, dest, proj_a, proj_b)


def grads_kernel(
    left_a, left_b, right_a, right_b, states_in, out_a, out_b, states_out,
    left, right, states, out, left_sem, right_sem, states_sem, out_sem,
):
    tiles, tile = out.shape[1:3]
    loads = []
    for which, (src_left, src_right) in enumerate(((left_a, right_a), (left_b, right_b))):
        loads.append((
            pltpu.make_async_copy(src_right, right.at[which], right_sem.at[which]),
            pltpu.make_async_copy(src_left, left.at[which], left_sem.at[which]),
        ))
    for pair in loads:
        for copy in pair:
            copy.start()
    bring = pltpu.make_async_copy(states_in, states, states_sem.at[0])
    give = pltpu.make_async_copy(states, states_out.at[0], states_sem.at[1])
    bring.start()

    def store(which, t):
        at = pl.ds(pl.multiple_of(t * tile, tile), tile)
        return pltpu.make_async_copy(
            out.at[which, t], (out_a, out_b)[which].at[0, at, :], out_sem.at[which, t]
        )

    for which in (0, 1):
        for copy in loads[which]:
            copy.wait()
        for t in range(tiles):
            part = left[which, :, t * tile : (t + 1) * tile]
            out[which, t] = left_product(part, right[which])
            store(which, t).start()
        if which == 0:
            bring.wait()
            give.start()
    for which in (0, 1):
        for t in range(tiles):
            store(which, t).wait()
    give.wait()


def grads(left_a, left_b, right_a, right_b, states):
    rows, cols = left_a.shape
    inner = right_a.shape[1]
    tokens, width = states.shape
    tile = min(cols, 2 * LANES)
    tiles = cols // tile
    bf16, f32 = jnp.bfloat16, jnp.float32
    dma = pltpu.SemaphoreType.DMA
    hbm = pl.BlockSpec(memory_space=pltpu.HBM)
    return pl.pallas_call(
        grads_kernel,
        out_shape=(
            jax.ShapeDtypeStruct((1, cols, inner), f32),
            jax.ShapeDtypeStruct((1, cols, inner), f32),
            jax.ShapeDtypeStruct((1, tokens, width), bf16),
        ),
        in_specs=[hbm] * 5,
        out_specs=[hbm] * 3,
        scratch_shapes=[
            pltpu.VMEM((2, rows, cols), bf16), pltpu.VMEM((2, rows, inner), bf16),
            pltpu.VMEM((tokens, width), bf16), pltpu.VMEM((2, tiles, tile, inner), f32),
            dma((2,)), dma((2,)), dma((2,)), dma((2, tiles)),
        ],
        compiler_params=pltpu.CompilerParams(vmem_limit_bytes=62 * 2**20),
        name="grads",
    )(left_a, left_b, right_a, right_b, states)


def per_device(states, gains, proj_a, proj_b, cotangent, src_len, tgt_len, dest):
    n = lax.axis_size("dp")
    m = lax.axis_size("mp")
    _, tokens, width = states.shape
    inner = proj_a.shape[2]
    args = (states, gains, proj_a, proj_b, cotangent, src_len, tgt_len, dest)
    if not fused_fits(n, m, src_len.shape[1], tokens, width, inner):
        return stepwise(*args)
    result, grad_first, grad_second, mine_a, mine_b = fused(n, m, *args)
    rows = n * tokens
    grad_a, grad_b, grad_states = grads(
        mine_a.reshape(rows, -1), mine_b.reshape(rows, -1),
        grad_first.reshape(rows, -1), grad_second.reshape(rows, -1), result,
    )
    return (grad_states, grad_a, grad_b)


def solution(mesh):
    return jax.shard_map(
        per_device,
        mesh=mesh,
        in_specs=(
            P("section", "dp", None),
            P("section", None),
            P("section", None, "mp"),
            P("section", None, "mp"),
            P("dp", None),
            P(),
            P(),
            P(),
        ),
        out_specs=(P("section", "dp", None), P("section", "dp", "mp"), P("section", "dp", "mp")),
        check_vma=False,
    )
```

```python
import functools

import jax
import jax.numpy as jnp
from jax import lax
from jax.experimental import pallas as pl
from jax.experimental.pallas import tpu as pltpu
from jax.sharding import PartitionSpec as P

HEAD_DIM = 64
LANES = 128
EPS = 1e-06
MAX_LEN = 16
MESH = pl.DeviceIdType.MESH


def rms_forward(states_row, gain):
    xf = states_row.astype(jnp.float32)
    scale = lax.rsqrt(jnp.mean(xf * xf, axis=-1, keepdims=True) + EPS)
    return (xf, scale, (xf * scale * gain).astype(jnp.bfloat16))


def left_product(left, right):
    return lax.dot_general(
        left, right, (((0,), (0,)), ((), ())), preferred_element_type=jnp.float32
    )


def right_product(rows, weight):
    return lax.dot_general(
        rows, weight, (((1,), (1,)), ((), ())), preferred_element_type=jnp.float32
    )


def sequence_of(lengths, names, tokens):
    slot = jnp.arange(lengths.shape[1], dtype=jnp.int32)
    before = slot[:, None] < slot[None, :]
    starts = jnp.sum(jnp.where(before[None], lengths[:, :, None], 0), axis=1)
    place = jnp.arange(tokens, dtype=jnp.int32)[None, :, None]
    offset = place - starts[:, None, :]
    inside = (offset >= 0) & (offset < lengths[:, None, :])
    return jnp.sum(jnp.where(inside, names[:, None, :], 0), axis=-1).reshape(-1)


def attend_piece(encoder, p, group, id_col, id_row, own, other, out_a, out_b, acc_a, acc_b):
    n, tokens, width = own.shape[1:]
    half = width // 2
    rows = n * tokens
    blocks = n // group
    lane = lax.broadcasted_iota(jnp.int32, (1, LANES), 1) // HEAD_DIM
    zero = jnp.zeros((), jnp.bfloat16)
    f32 = jnp.float32

    def cut(ref, which, c, at):
        lo = pl.multiple_of(which * half + c * LANES, LANES)
        return ref[p, at, :, pl.ds(lo, LANES)].reshape(-1, LANES)

    every = pl.ds(0, n)

    @pl.loop(0, half // LANES)
    def _(c):
        out_cols = pl.ds(pl.multiple_of(p * half + c * LANES, LANES), LANES)

        @pl.when(encoder)
        def _():
            keys, values = cut(own, 0, c, every), cut(own, 1, c, every)
            if blocks > 1:
                acc_a[...] = jnp.zeros_like(acc_a)
                acc_b[...] = jnp.zeros_like(acc_b)

            def block(b):
                at = pl.ds(b * group, group)
                query, dout = cut(other, 0, c, at), cut(other, 1, c, at)
                mask = id_col[...].reshape(rows, 1) == id_row[b]
                dk, dv = None, None
                for h in range(LANES // HEAD_DIM):
                    qh = jnp.where(lane == h, query, zero)
                    dh = jnp.where(lane == h, dout, zero)
                    expo = jnp.exp(jnp.where(mask, right_product(keys, qh), -jnp.inf))
                    weight = expo * (1.0 / jnp.sum(expo, axis=0, keepdims=True))
                    dweight = right_product(values, dh)
                    total = jnp.sum(weight * dweight, axis=0, keepdims=True)
                    dscore = (weight * (dweight - total)).astype(jnp.bfloat16)
                    pk = jnp.dot(dscore, qh, preferred_element_type=f32)
                    pv = jnp.dot(weight.astype(jnp.bfloat16), dh, preferred_element_type=f32)
                    dk = pk if dk is None else dk + pk
                    dv = pv if dv is None else dv + pv
                if blocks == 1:
                    out_a[:, :, out_cols] = dk.astype(jnp.bfloat16).reshape(n, tokens, LANES)
                    out_b[:, :, out_cols] = dv.astype(jnp.bfloat16).reshape(n, tokens, LANES)
                else:
                    acc_a[...] += dk
                    acc_b[...] += dv

            if blocks == 1:
                block(0)
            else:
                pl.loop(0, blocks)(block)
                out_a[:, :, out_cols] = acc_a[...].astype(jnp.bfloat16).reshape(n, tokens, LANES)
                out_b[:, :, out_cols] = acc_b[...].astype(jnp.bfloat16).reshape(n, tokens, LANES)

        @pl.when(jnp.logical_not(encoder))
        def _():
            keys, values = cut(other, 0, c, every), cut(other, 1, c, every)

            def block(b):
                at = pl.ds(b * group, group)
                query, dout = cut(own, 0, c, at), cut(own, 1, c, at)
                ids = id_col[at, :, :].reshape(group * tokens, 1)
                mask = None
                dq, att = None, None
                for h in range(LANES // HEAD_DIM):
                    kh = jnp.where(lane == h, keys, zero)
                    vh = jnp.where(lane == h, values, zero)
                    score = right_product(query, kh)
                    if mask is None:
                        span = group * tokens
                        mask = jnp.concatenate(
                            [ids == id_row[i] for i in range(rows // span)], axis=1
                        )
                    expo = jnp.exp(jnp.where(mask, score, -jnp.inf))
                    weight = expo * (1.0 / jnp.sum(expo, axis=1, keepdims=True))
                    dweight = right_product(dout, vh)
                    total = jnp.sum(weight * dweight, axis=1, keepdims=True)
                    dscore = (weight * (dweight - total)).astype(jnp.bfloat16)
                    pq = jnp.dot(dscore, kh, preferred_element_type=f32)
                    pa = jnp.dot(weight.astype(jnp.bfloat16), vh, preferred_element_type=f32)
                    dq = pq if dq is None else dq + pq
                    att = pa if att is None else att + pa
                shape = (group, tokens, LANES)
                out_a[at, :, out_cols] = dq.astype(jnp.bfloat16).reshape(shape)
                out_b[at, :, out_cols] = att.astype(jnp.bfloat16).reshape(shape)

            if blocks == 1:
                block(0)
            else:
                pl.loop(0, blocks)(block)


def forward_kernel(
    n, m, group, normed, second, id_col, id_row, proj_a, proj_b,
    out_a, out_b, mine_a, mine_b,
    wbuf, paired, own, other, acc_a, acc_b, wsem,
    line_send, line_recv, sec_send, sec_recv, za_send, za_recv, mp_send, mp_recv, loc_sem,
):
    me = lax.axis_index("dp")
    col = lax.axis_index("mp")
    sec = lax.axis_index("section")
    tokens, width = normed.shape
    pieces = wbuf.shape[1]
    half = wbuf.shape[3]
    part = tokens // m
    cols = width // n

    def weight_copy(which, p):
        src = (proj_a, proj_b)[which]
        return pltpu.make_async_copy(
            src.at[0, :, pl.ds(p * half, half)], wbuf.at[which, p], wsem.at[which, p]
        )

    for p in range(pieces):
        for which in (0, 1):
            weight_copy(which, p).start()

    barrier = pltpu.get_barrier_semaphore()
    for j in range(1, n):
        pl.semaphore_signal(
            barrier, inc=1, device_id={"dp": lax.rem(me + j, n)}, device_id_type=MESH
        )
    for j in range(1, m):
        pl.semaphore_signal(
            barrier, inc=1, device_id={"mp": lax.rem(col + j, m)}, device_id_type=MESH
        )
    pl.semaphore_signal(barrier, inc=1, device_id={"section": 1 - sec}, device_id_type=MESH)
    pl.semaphore_wait(barrier, n + m - 1)

    band = pl.ds(pl.multiple_of(col * part, part), part)

    def line_copy(way, s, p):
        chunk = me - s if way == 0 else me + s
        target = me + 1 if way == 0 else me - 1
        src = paired.at[p] if s == 0 else own.at[p, chunk]
        return pltpu.make_async_remote_copy(
            src_ref=src, dst_ref=own.at[p, chunk],
            send_sem=line_send.at[way, s, p], recv_sem=line_recv.at[way, s, p],
            device_id={"dp": target}, device_id_type=MESH,
        )

    def line_ok(way, s):
        if way == 0:
            return jnp.logical_and(me - s >= 0, me < n - 1)
        return jnp.logical_and(me + s <= n - 1, me > 0)

    def got(way, s):
        return me - 1 - s >= 0 if way == 0 else me + 1 + s <= n - 1

    def sec_copy(chunk, p, src):
        return pltpu.make_async_remote_copy(
            src_ref=src, dst_ref=other.at[p, chunk],
            send_sem=sec_send.at[chunk, p], recv_sem=sec_recv.at[chunk, p],
            device_id={"section": 1 - sec}, device_id_type=MESH,
        )

    def za_copy(which, j):
        src, dst = ((normed, mine_a), (second, mine_b))[which]
        peer = lax.rem(me + j, n)
        return pltpu.make_async_remote_copy(
            src_ref=src.at[band, pl.ds(pl.multiple_of(peer * cols, cols), cols)],
            dst_ref=dst.at[me, band, :],
            send_sem=za_send.at[which, j], recv_sem=za_recv.at[which, j],
            device_id={"dp": peer}, device_id_type=MESH,
        )

    def mp_copy(which, j):
        dst = (mine_a, mine_b)[which]
        return pltpu.make_async_remote_copy(
            src_ref=dst.at[:, band, :], dst_ref=dst.at[:, band, :],
            send_sem=mp_send.at[which, j], recv_sem=mp_recv.at[which, j],
            device_id={"mp": lax.rem(col + j, m)}, device_id_type=MESH,
        )

    def local(which):
        src, dst = ((normed, mine_a), (second, mine_b))[which]
        return pltpu.make_async_copy(
            src.at[band, pl.ds(pl.multiple_of(me * cols, cols), cols)],
            dst.at[me, band, :], loc_sem.at[which],
        )

    def keep(p):
        return pltpu.make_async_copy(paired.at[p], own.at[p, me], loc_sem.at[2 + p])

    def second_too(fn):
        fn(0)
        pl.when(sec == 1)(lambda: fn(1))

    for j in range(1, n):
        second_too(lambda which: za_copy(which, j).start())
    second_too(lambda which: local(which).start())

    for p in range(pieces):
        for which in (0, 1):
            weight_copy(which, p).wait()
            rows_in = (normed, second)[which]
            paired[p, :, which * half : (which + 1) * half] = jnp.dot(
                rows_in[...], wbuf[which, p], preferred_element_type=jnp.float32
            ).astype(jnp.bfloat16)
        for way in (0, 1):
            pl.when(line_ok(way, 0))(lambda way=way, p=p: line_copy(way, 0, p).start())
        sec_copy(me, p, paired.at[p]).start()
        keep(p).start()

    def spread(which):
        local(which).wait()
        for j in range(1, n):
            za_copy(which, j).wait_recv()
        for j in range(1, m):
            mp_copy(which, j).start()

    second_too(spread)

    for wave in range(pieces + n - 2):
        for s in range(max(0, wave - pieces + 1), min(n - 1, wave + 1)):
            p = wave - s
            for way in (0, 1):

                @pl.when(got(way, s))
                def _():
                    line_copy(way, s, p).wait_recv()
                    chunk = me - 1 - s if way == 0 else me + 1 + s
                    if s + 1 < n - 1:
                        pl.when(line_ok(way, s + 1))(
                            lambda: line_copy(way, s + 1, p).start()
                        )
                    sec_copy(chunk, p, own.at[p, chunk]).start()

        p = wave - (n - 2)
        if p >= 0:
            keep(p).wait()
            for c in range(n):
                sec_copy(c, p, own.at[p, c]).wait_recv()
            attend_piece(
                sec == 0, p, group, id_col, id_row, own, other, out_a, out_b, acc_a, acc_b
            )

    def finish(which):
        for j in range(1, n):
            za_copy(which, j).wait_send()
        for j in range(1, m):
            mp_copy(which, j).wait()

    second_too(finish)
    for p in range(pieces):
        for s in range(n - 1):
            for way in (0, 1):
                pl.when(line_ok(way, s))(
                    lambda way=way, s=s, p=p: line_copy(way, s, p).wait_send()
                )
        for c in range(n):
            sec_copy(c, p, own.at[p, c]).wait_send()


def forward(n, m, normed, second, id_c, id_r, proj_a, proj_b):
    tokens, width = normed.shape
    inner = proj_a.shape[2]
    half = 2 * LANES
    pieces = inner // half
    rows = n * tokens
    group = max(1, min(n, 512 * 512 // (rows * tokens)))
    blocks = n // group
    grad = jax.ShapeDtypeStruct((n, tokens, inner), jnp.bfloat16)
    mine = jax.ShapeDtypeStruct((n, tokens, width // n), jnp.bfloat16)
    acc = (rows, LANES) if blocks > 1 else (8, LANES)
    dma = pltpu.SemaphoreType.DMA
    vmem = pl.BlockSpec(memory_space=pltpu.VMEM)
    anyw = pl.BlockSpec(memory_space=pltpu.HBM)
    bf16 = jnp.bfloat16
    return pl.pallas_call(
        functools.partial(forward_kernel, n, m, group),
        out_shape=(grad, grad, mine, mine),
        in_specs=[vmem] * 4 + [anyw] * 2,
        out_specs=[vmem, vmem, anyw, anyw],
        scratch_shapes=[
            pltpu.VMEM((2, pieces, width, half), bf16),
            pltpu.VMEM((pieces, tokens, 2 * half), bf16),
            pltpu.VMEM((pieces, n, tokens, 2 * half), bf16),
            pltpu.VMEM((pieces, n, tokens, 2 * half), bf16),
            pltpu.VMEM(acc, jnp.float32), pltpu.VMEM(acc, jnp.float32),
            dma((2, pieces)),
            dma((2, n, pieces)), dma((2, n, pieces)), dma((n, pieces)), dma((n, pieces)),
            dma((2, n)), dma((2, n)), dma((2, m)), dma((2, m)), dma((2 + pieces,)),
        ],
        compiler_params=pltpu.CompilerParams(
            collective_id=0, has_side_effects=True, vmem_limit_bytes=67000000
        ),
        name="forward",
    )(normed, second, id_c.reshape(n, tokens, 1), id_r.reshape(blocks, 1, rows // blocks),
      proj_a, proj_b)


def reduce_kernel(
    m, grad_a, grad_b, proj_a, proj_b, x_ref, gain_ref, result,
    left, wbuf, total, mine, partial, landed, gsem, wsem, send, recv,
):
    me = lax.axis_index("dp")
    col = lax.axis_index("mp")
    encoder = lax.axis_index("section") == 0
    tokens = x_ref.shape[0]
    part = tokens // m
    chunks, step = wbuf.shape[1:3]

    def left_copy(which):
        return pltpu.make_async_copy(
            (grad_a, grad_b)[which].at[me], left.at[which], gsem.at[which]
        )

    def weight_copy(which, c):
        return pltpu.make_async_copy(
            (proj_a, proj_b)[which].at[0, pl.ds(c * step, step), :],
            wbuf.at[which, c], wsem.at[which, c],
        )

    left_copy(0).start()
    pl.when(encoder)(lambda: left_copy(1).start())
    for c in range(chunks):
        weight_copy(0, c).start()
        pl.when(encoder)(lambda c=c: weight_copy(1, c).start())

    barrier = pltpu.get_barrier_semaphore()
    for j in range(1, m):
        pl.semaphore_signal(
            barrier, inc=1, device_id={"mp": lax.rem(col + j, m)}, device_id_type=MESH
        )
    pl.semaphore_wait(barrier, m - 1)

    def scatter(j, c):
        peer = lax.rem(col + j, m)
        rows = pl.ds(pl.multiple_of(peer * part, part), part)
        at = pl.ds(c * step, step)
        return pltpu.make_async_remote_copy(
            src_ref=partial.at[rows, at], dst_ref=landed.at[j, :, at],
            send_sem=send.at[j, c], recv_sem=recv.at[j, c],
            device_id={"mp": peer}, device_id_type=MESH,
        )

    band = pl.ds(pl.multiple_of(col * part, part), part)
    left_copy(0).wait()
    pl.when(encoder)(lambda: left_copy(1).wait())
    for c in range(chunks):
        weight_copy(0, c).wait()
        total[...] = right_product(left[0], wbuf[0, c])

        @pl.when(encoder)
        def _():
            weight_copy(1, c).wait()
            total[...] += right_product(left[1], wbuf[1, c])

        partial[:, c * step : (c + 1) * step] = total[...].astype(jnp.bfloat16)
        mine[:, c * step : (c + 1) * step] = total[band, :]
        for j in range(1, m):
            scatter(j, c).start()
    x = x_ref[band, :].astype(jnp.float32)
    scale = lax.rsqrt(jnp.mean(x * x, axis=-1, keepdims=True) + EPS)
    for j in range(1, m):
        for c in range(chunks):
            scatter(j, c).wait_recv()
    dnorm = mine[...]
    for j in range(1, m):
        dnorm = dnorm + landed[j].astype(jnp.float32)
    upper = gain_ref[...] * dnorm
    inner = jnp.mean(x * upper, axis=-1, keepdims=True)
    result[...] = (scale * upper - x * scale * scale * scale * inner).astype(jnp.bfloat16)
    for j in range(1, m):
        for c in range(chunks):
            scatter(j, c).wait_send()


def reduce_norm(m, grad_a, grad_b, proj_a, proj_b, states, gain):
    tokens, width = states.shape
    inner = proj_a.shape[2]
    part = tokens // m
    step = 4 * LANES
    chunks = width // step
    dma = pltpu.SemaphoreType.DMA
    bf16, f32 = jnp.bfloat16, jnp.float32
    vmem = pl.BlockSpec(memory_space=pltpu.VMEM)
    return pl.pallas_call(
        functools.partial(reduce_kernel, m),
        out_shape=jax.ShapeDtypeStruct((part, width), bf16),
        in_specs=[pl.BlockSpec(memory_space=pltpu.HBM)] * 4 + [vmem] * 2,
        out_specs=vmem,
        scratch_shapes=[
            pltpu.VMEM((2, tokens, inner), bf16),
            pltpu.VMEM((2, chunks, step, inner), bf16),
            pltpu.VMEM((tokens, step), f32),
            pltpu.VMEM((part, width), f32),
            pltpu.VMEM((tokens, width), bf16),
            pltpu.VMEM((m, part, width), bf16),
            dma((2,)), dma((2, chunks)), dma((m, chunks)), dma((m, chunks)),
        ],
        compiler_params=pltpu.CompilerParams(
            collective_id=1, has_side_effects=True, vmem_limit_bytes=66500000
        ),
        name="reduce_norm",
    )(grad_a, grad_b, proj_a, proj_b, states, gain)


def stepwise(states, gains, proj_a, proj_b, cotangent, src_len, tgt_len, dest):
    encoder = lax.axis_index("section") == 0
    member = lax.axis_index("dp")
    n = lax.axis_size("dp")
    m = lax.axis_size("mp")
    gain = gains[0]
    weight_a = proj_a[0]
    weight_b = proj_b[0]
    tokens = states.shape[1]
    _, _, normed = rms_forward(states[0], gain)
    second_left = jnp.where(encoder, normed, cotangent)
    rows = n * tokens
    seqs = tgt_len.shape[1]
    names = jnp.arange(n * seqs, dtype=jnp.int32).reshape(n, seqs)
    id_c = sequence_of(
        jnp.where(encoder, src_len, tgt_len), jnp.where(encoder, dest, names), tokens
    )
    id_r = sequence_of(
        jnp.where(encoder, tgt_len, src_len), jnp.where(encoder, names, dest), tokens
    )
    grad_first, grad_second, mine_a, mine_b = forward(
        n, m, normed, second_left, id_c, id_r, proj_a, proj_b
    )
    mine = reduce_norm(m, grad_first, grad_second, proj_a, proj_b, states[0], gains)
    col = lax.axis_index("mp")
    landed = [mine] + [
        lax.ppermute(mine, "mp", [(i, (i + j) % m) for i in range(m)]) for j in range(1, m)
    ]
    mine_a = mine_a.reshape(rows, -1)
    mine_b = jnp.where(encoder, mine_a, mine_b.reshape(rows, -1))
    grad_a = left_product(mine_a, grad_first.reshape(rows, -1))
    grad_b = left_product(mine_b, grad_second.reshape(rows, -1))
    bands = []
    for b in range(m):
        band = landed[0]
        for j in range(1, m):
            band = jnp.where(col == (b + j) % m, landed[j], band)
        bands.append(band)
    grad_states = jnp.concatenate(bands, axis=0)
    return (grad_states[None], grad_a[None], grad_b[None])


def packed_ids(lengths, names, tokens):
    n, seqs = lengths.shape
    place = lax.broadcasted_iota(jnp.int32, (n, tokens), 1)
    start = jnp.zeros((n, 1), jnp.int32)
    ids = jnp.zeros((n, tokens), jnp.int32)
    for i in range(seqs):
        length = lengths[:, i : i + 1]
        offset = place - start
        ids = jnp.where((offset >= 0) & (offset < length), names(i), ids)
        start = start + length
    return (ids + 1).astype(jnp.float32)


def fused_kernel(
    n, m, x_hbm, cot_hbm, gain_hbm, src_hbm, tgt_hbm, dest_hbm, proj_a, proj_b,
    result, out_a, out_b, mine_a, mine_b,
    gain, src_len, tgt_len, dest, rest, x, xall, wbuf, own, other, grad_a, grad_b, id_col, id_row, pick, id_far, far, total, partial, landed,
    gate, in_sem, wsem, loc_sem, out_sem, zx_send, zx_recv, px_send, px_recv, line_send, line_recv,
    sec_send, sec_recv, za_send, za_recv, sl_send, sl_recv, rs_send, rs_recv, ag_send, ag_recv,
):
    me = lax.axis_index("dp")
    col = lax.axis_index("mp")
    sec = lax.axis_index("section")
    encoder = sec == 0
    decoder = sec == 1
    tokens, width = x.shape
    pieces, half = wbuf.shape[1], wbuf.shape[3]
    part = tokens // m
    cols = width // n
    rows = n * tokens
    step = 4 * LANES
    chunks = width // step
    quarter = width // pieces
    hops = (n - 1) * pieces
    seqs = src_len.shape[1]
    cap = far.shape[0]
    f32, bf16 = jnp.float32, jnp.bfloat16
    spare = lax.rem(me + 1, n)
    near_x = col + 1 - 2 * lax.rem(col, 2)
    near_y = lax.rem(col + 2, m)
    band = pl.ds(pl.multiple_of(col * part, part), part)
    lane = lax.broadcasted_iota(jnp.int32, (1, LANES), 1) // HEAD_DIM
    zero = jnp.zeros((), bf16)

    def remote(src, dst, send, recv, **device):
        return pltpu.make_async_remote_copy(
            src_ref=src, dst_ref=dst, send_sem=send, recv_sem=recv,
            device_id=device, device_id_type=MESH,
        )

    def weight_copy(which, p):
        src = (proj_a, proj_b)[which]
        return pltpu.make_async_copy(
            src.at[0, :, pl.ds(pl.multiple_of(p * half, half), half)],
            wbuf.at[which, p], wsem.at[which, p],
        )

    x_copy = pltpu.make_async_copy(x_hbm.at[0], x, in_sem.at[0])
    cot_copy = pltpu.make_async_copy(cot_hbm, xall.at[spare], in_sem.at[1])
    small_copies = [
        pltpu.make_async_copy(src, dst, in_sem.at[2 + i])
        for i, (src, dst) in enumerate(
            ((gain_hbm, gain), (src_hbm, src_len), (tgt_hbm, tgt_len), (dest_hbm, dest))
        )
    ]
    x_copy.start()
    for copy in small_copies:
        copy.start()
    pl.when(decoder)(cot_copy.start)
    for p in range(pieces):
        for which in (0, 1):
            weight_copy(which, p).start()

    barrier = pltpu.get_barrier_semaphore()
    for j in range(1, n):
        pl.semaphore_signal(
            barrier, inc=1, device_id={"dp": lax.rem(me + j, n)}, device_id_type=MESH
        )
    for j in range(1, m):
        pl.semaphore_signal(
            barrier, inc=1, device_id={"mp": lax.rem(col + j, m)}, device_id_type=MESH
        )
    pl.semaphore_signal(barrier, inc=1, device_id={"section": 1 - sec}, device_id_type=MESH)
    x_copy.wait()
    for copy in small_copies:
        copy.wait()
    group = min(tokens, 16)

    @pl.loop(0, tokens // group)
    def _(r):
        at = pl.ds(pl.multiple_of(r * group, group), group)
        xf = x[at, :].astype(f32)
        scale = lax.rsqrt(jnp.mean(xf * xf, axis=-1, keepdims=True) + EPS)
        xall[me, at, :] = (xf * scale * gain[...]).astype(bf16)

    pl.semaphore_wait(barrier, n + m - 1)

    def source(way, s):
        return me - (1 - 2 * way) * (1 + s)

    def got(way, s):
        src = source(way, s)
        return jnp.logical_and(src >= 0, src < n)

    def line_ok(way, s):
        chunk = source(way, s - 1)
        target = me + 1 - 2 * way
        inside = jnp.logical_and(chunk >= 0, chunk < n)
        return jnp.logical_and(inside, jnp.logical_and(target >= 0, target < n))

    def span(q):
        return pl.ds(pl.multiple_of(q * quarter, quarter), quarter)

    def zx_copy(way, s, q):
        ref = xall.at[source(way, s - 1), band, span(q)]
        return remote(
            ref, ref, zx_send.at[way, s, q], zx_recv.at[way, s, q], dp=me + 1 - 2 * way
        )

    def line_copy(way, s, p):
        ref = own.at[p, source(way, s - 1)]
        return remote(
            ref, ref, line_send.at[way, s, p], line_recv.at[way, s, p], dp=me + 1 - 2 * way
        )

    def sec_copy(chunk, p):
        return remote(
            own.at[p, chunk], other.at[p, chunk],
            sec_send, sec_recv.at[p], section=1 - sec,
        )

    def sec_all(p):
        return remote(own.at[p], other.at[p], sec_send, sec_recv.at[p], section=1 - sec)

    def plane(view, send, recv, kind):
        small = part // 2
        start = (col * part, col * part, near_x * part, near_y * part + small)[kind]
        size = (part, part, small, small)[kind]
        target = (near_x, near_y, near_y, near_x)[kind]
        ref = view(pl.ds(pl.multiple_of(start, small), size))
        return remote(ref, ref, send, recv.at[kind], mp=target)

    def px_copy(src, q, kind):
        return plane(
            lambda at: xall.at[src, at, span(q)], px_send.at[src], px_recv.at[src, q], kind
        )

    def za_copy(which, j):
        peer = lax.rem(me + j, n)
        src = xall.at[(me, spare)[which]]
        return remote(
            src.at[band, pl.ds(pl.multiple_of(peer * cols, cols), cols)],
            (mine_a, mine_b)[which].at[me, band, :],
            za_send.at[which, j], za_recv.at[which, j], dp=peer,
        )

    def sl_copy(which, j, kind):
        block = lax.rem(me + n - j, n)
        return plane(
            lambda at: (mine_a, mine_b)[which].at[block, at, :],
            sl_send.at[which, j], sl_recv.at[which, j], kind,
        )

    def scatter(j, d):
        peer = lax.rem(col + j, m)
        at = pl.ds(pl.multiple_of(d * step, step), step)
        return remote(
            partial.at[pl.ds(pl.multiple_of(peer * part, part), part), at],
            landed.at[j, :, at], rs_send, rs_recv.at[j], mp=peer,
        )

    def scatter_all(j):
        peer = lax.rem(col + j, m)
        return remote(
            partial.at[pl.ds(0, part), :], landed.at[j], rs_send, rs_recv.at[j], mp=peer
        )

    def gather(kind):
        if kind > 1:
            return plane(lambda at: result.at[at, :], ag_send.at[kind], ag_recv, kind)
        return remote(
            rest, result.at[band, :], ag_send.at[kind], ag_recv.at[kind],
            mp=(near_x, near_y)[kind],
        )

    keep_rest = pltpu.make_async_copy(rest, result.at[band, :], loc_sem.at[2])

    my_cols = pl.ds(pl.multiple_of(me * cols, cols), cols)

    def keep_slice(which):
        src = xall.at[(me, spare)[which]]
        return pltpu.make_async_copy(
            src.at[:, my_cols], (mine_a, mine_b)[which].at[me], loc_sem.at[which]
        )

    def keep_all(which):
        return pltpu.make_async_copy(
            xall.at[:, :, my_cols], (mine_a, mine_b)[which], loc_sem.at[which]
        )

    def grad_out(which, p):
        of = pl.ds(pl.multiple_of(p * half, half), half)
        return pltpu.make_async_copy(
            (grad_a, grad_b)[which].at[:, :, of], (out_a, out_b)[which].at[:, :, of],
            out_sem.at[which, p],
        )

    @pl.when(decoder)
    def _():
        cot_copy.wait()
        for j in range(1, n):
            za_copy(1, j).start()

    @pl.when(encoder)
    def _():
        for q in range(pieces):
            for way in (0, 1):
                pl.when(line_ok(way, 0))(lambda way=way, q=q: zx_copy(way, 0, q).start())

    @pl.when(decoder)
    def _():
        for j in range(1, n):
            za_copy(0, j).start()
        for which in (0, 1):
            keep_slice(which).start()

    src_ids = packed_ids(src_len, lambda i: dest[:, i : i + 1], tokens)
    device = lax.broadcasted_iota(jnp.int32, (n, 1), 0)
    tgt_ids = packed_ids(tgt_len, lambda i: device * seqs + i, tokens)
    id_row[...] = jnp.where(encoder, tgt_ids, src_ids)
    near_ids = jnp.where(encoder, src_ids, tgt_ids)
    for b in range(n):
        id_col[b] = jnp.transpose(jnp.broadcast_to(near_ids[b : b + 1, :], (LANES, tokens)))
    flat = jnp.concatenate([id_row[b : b + 1, :] for b in range(n)], axis=1)
    flat = jnp.broadcast_to(flat, (16, rows)).astype(bf16)
    before = lax.broadcasted_iota(jnp.int32, (rows, rows), 0)
    before = before < lax.broadcasted_iota(jnp.int32, (rows, rows), 1)
    before = jnp.where(before, 1.0, 0.0).astype(bf16)
    slot = lax.broadcasted_iota(jnp.int32, (cap, rows), 0).astype(f32)
    for b in range(n):
        member = jnp.concatenate(
            [
                jnp.max(
                    jnp.where(id_col[b] == id_row[c : c + 1, :], 1.0, 0.0), axis=0, keepdims=True
                )
                for c in range(n)
            ],
            axis=1,
        )
        rank = jnp.dot(
            jnp.broadcast_to(member, (16, rows)).astype(bf16), before, preferred_element_type=f32
        )[0:1, :]
        key = jnp.where(member > 0.0, rank, -1.0)
        chosen = jnp.where(key == slot, 1.0, 0.0).astype(bf16)
        pick[b] = chosen
        id_far[b] = right_product(flat, chosen)

    def project(p, blk_a, blk_b, out):
        for which in (0, 1):
            own[p, out, :, which * half : (which + 1) * half] = jnp.dot(
                xall[(blk_a, blk_b)[which]], wbuf[which, p], preferred_element_type=f32
            ).astype(bf16)
        sec_copy(out, p).start()

    def x_line(i):
        s, q = i // pieces, i % pieces
        for way in (0, 1):

            @pl.when(got(way, s))
            def _():
                zx_copy(way, s, q).wait_recv()
                pl.when(line_ok(way, s + 1))(lambda: zx_copy(way, s + 1, q).start())
                for kind in (0, 1):
                    px_copy(source(way, s), q, kind).start()

    def x_near(i):
        s, q = i // pieces, i % pieces
        for way in (0, 1):

            @pl.when(got(way, s))
            def _():
                for kind in (0, 1):
                    px_copy(source(way, s), q, kind).wait_recv()
                    px_copy(source(way, s), q, 2 + kind).start()

    def x_done(i):
        s, q = i // pieces, i % pieces
        for way in (0, 1):

            @pl.when(got(way, s))
            def _():
                for kind in (2, 3):
                    px_copy(source(way, s), q, kind).wait_recv()

    def x_work(i):
        @pl.loop(0, 2)
        def _(way):
            src = source(way, i // pieces)
            pl.when(got(way, i // pieces))(lambda: project(i % pieces, src, src, src))

    @pl.loop(0, pieces)
    def _(p):
        for which in (0, 1):
            weight_copy(which, p).wait()
        project(p, me, lax.rem(me + sec, n), me)

    heads = LANES // HEAD_DIM

    def stack(near):
        return jnp.concatenate([jnp.where(lane == h, near, zero) for h in range(heads)], axis=0)

    def merge(left, right):
        whole = jnp.dot(left.reshape(-1, cap), right, preferred_element_type=f32)
        whole = whole.reshape(heads, tokens, LANES)
        picked = whole[0]
        for h in range(1, heads):
            picked = jnp.where(lane == h, whole[h], picked)
        return picked.astype(bf16)

    def unit(axis, p, blk):
        far[...] = jnp.dot(
            pick[blk], other[p].reshape(rows, 2 * half), preferred_element_type=f32
        ).astype(bf16)
        mask = jnp.concatenate(
            [
                id_col[blk] == id_far[blk, 0:1, c * LANES : (c + 1) * LANES]
                for c in range(cap // LANES)
            ],
            axis=1,
        )

        @pl.loop(0, half // LANES, unroll=True)
        def _(c):
            lo = pl.ds(pl.multiple_of(c * LANES, LANES), LANES)
            hi = pl.ds(pl.multiple_of(half + c * LANES, LANES), LANES)
            at = pl.ds(pl.multiple_of(p * half + c * LANES, LANES), LANES)
            near_a, near_b = own[p, blk, :, lo], own[p, blk, :, hi]
            far_a, far_b = far[:, lo], far[:, hi]
            score = right_product(stack(near_a), far_a).reshape(heads, tokens, cap)
            expo = jnp.exp(jnp.where(mask[None], score, -jnp.inf))
            norm = jnp.sum(expo, axis=axis + 1, keepdims=True)
            weight = expo * (1.0 / jnp.where(norm == 0.0, 1.0, norm))
            dweight = right_product(stack(near_b), far_b).reshape(heads, tokens, cap)
            shift = jnp.sum(weight * dweight, axis=axis + 1, keepdims=True)
            dscore = (weight * (dweight - shift)).astype(bf16)
            grad_a[blk, :, at] = merge(dscore, far_a)
            grad_b[blk, :, at] = merge(weight.astype(bf16), far_b)

    def others(axis, p):
        @pl.loop(1, n)
        def _(j):
            unit(axis, p, lax.rem(me + j, n))

    def ready(p):
        sec_all(p).wait_recv()

    def reduce_own(which_all):
        @pl.loop(0, chunks, unroll=2)
        def _(d):
            at = pl.ds(pl.multiple_of(d * step, step), step)
            acc = None
            for which in which_all:
                for p in range(pieces):
                    left = (grad_a, grad_b)[which][me, :, p * half : (p + 1) * half]
                    term = right_product(left, wbuf[which, p, at, :])
                    acc = term if acc is None else acc + term
            total[:, at] = acc
            partial[:, at] = acc.astype(bf16)
            for j in range(1, m):
                scatter(j, d).start()

    def finish_own():
        xf = x[band, :].astype(f32)
        scale = lax.rsqrt(jnp.mean(xf * xf, axis=-1, keepdims=True) + EPS)
        for j in range(1, m):
            scatter_all(j).wait_recv()
        dnorm = total[band, :]
        for j in range(1, m):
            dnorm = dnorm + landed[j].astype(f32)
        upper = gain[...] * dnorm
        inner = jnp.mean(xf * upper, axis=-1, keepdims=True)
        rest[...] = (scale * upper - xf * scale * scale * scale * inner).astype(bf16)
        gather(0).start()
        gather(1).start()
        keep_rest.start()

    def relay_own():
        for kind in (0, 1):
            gather(kind).wait_recv()
            gather(2 + kind).start()

    def wave(w):
        for s in range(max(0, w - pieces + 1), min(n - 1, w + 1)):
            p = w - s
            for way in (0, 1):

                @pl.when(got(way, s))
                def _():
                    line_copy(way, s, p).wait_recv()
                    if s + 1 < n - 1:
                        pl.when(line_ok(way, s + 1))(
                            lambda: line_copy(way, s + 1, p).start()
                        )
                    sec_copy(source(way, s), p).start()

    def drain_source():
        @pl.loop(0, hops)
        def _(i):
            s, q = i // pieces, i % pieces
            for way in (0, 1):
                pl.when(line_ok(way, s))(lambda way=way: zx_copy(way, s, q).wait_send())

                @pl.when(jnp.logical_and(got(way, s), q == 0))
                def _():
                    src = source(way, s)
                    ref = xall.at[src, pl.ds(0, 3 * part), :]
                    remote(
                        ref, ref, px_send.at[src], px_recv.at[src, 0, 0], mp=near_x
                    ).wait_send()

        for which in (0, 1):
            keep_all(which).wait()

    def drain_target():
        for which in (0, 1):
            keep_slice(which).wait()
            for j in range(1, n):
                za_copy(which, j).wait_send()
                ref = (mine_a, mine_b)[which].at[0, pl.ds(0, 3 * part), :]
                remote(
                    ref, ref, sl_send.at[which, j], sl_recv.at[which, j, 0], mp=near_x
                ).wait_send()
                for kind in (2, 3):
                    sl_copy(which, j, kind).wait_recv()
        for p in range(pieces):
            for s in range(n - 1):
                for way in (0, 1):
                    pl.when(line_ok(way, s))(
                        lambda way=way, s=s, p=p: line_copy(way, s, p).wait_send()
                    )

    def drain_section():
        remote(own, other, sec_send, sec_recv.at[0], section=1 - sec).wait_send()

    @pl.when(encoder)
    def _():
        lags = (0, 2, 5, 4 + pieces)

        @pl.loop(0, hops + lags[3])
        def _(i):
            for lag, stage in zip(lags, (x_line, x_near, x_done, x_work)):
                at = i - lag
                inside = jnp.logical_and(at >= 0, at < hops)
                pl.when(inside)(lambda stage=stage, at=at: stage(at))

            @pl.when(i == 1)
            def _():
                pl.semaphore_signal(
                    gate, inc=1, device_id={"section": 1 - sec}, device_id_type=MESH
                )

        for which in (0, 1):
            keep_all(which).start()

        @pl.loop(0, pieces)
        def _(p):
            ready(p)
            unit(0, p, me)

        reduce_own((0, 1))

        @pl.loop(0, pieces)
        def _(p):
            others(0, p)
            for which in (0, 1):
                grad_out(which, p).start()
            pl.when(p == 1)(finish_own)

            @pl.when(p == 2)
            def _():
                drain_source()
                drain_section()
                relay_own()


    @pl.when(decoder)
    def _():
        pl.semaphore_wait(gate, 1)
        for p in range(pieces):
            for way in (0, 1):
                pl.when(line_ok(way, 0))(
                    lambda way=way, p=p: line_copy(way, 0, p).start()
                )
        for w in range(pieces):
            wave(w)
        for which in (0, 1):
            for j in range(1, n):
                za_copy(which, j).wait_recv()
                for kind in (0, 1):
                    sl_copy(which, j, kind).start()

        @pl.loop(0, pieces)
        def _(p):
            ready(p)
            unit(1, p, me)
            for late in range(n - 2):
                pl.when(p == min(late, pieces - 1))(lambda late=late: wave(pieces + late))

        reduce_own((0,))
        for which in (0, 1):
            for j in range(1, n):
                for kind in (0, 1):
                    sl_copy(which, j, kind).wait_recv()
                    sl_copy(which, j, 2 + kind).start()
        @pl.loop(0, pieces)
        def _(p):
            others(1, p)
            for which in (0, 1):
                grad_out(which, p).start()
            pl.when(p == 1)(finish_own)

            @pl.when(p == 2)
            def _():
                drain_target()
                drain_section()
                relay_own()

    sent = pl.ds(0, (m - 1) * part)
    remote(
        partial.at[sent, :], partial.at[sent, :], rs_send, rs_recv.at[0],
        mp=lax.rem(col + 1, m),
    ).wait_send()
    for kind in range(4):
        gather(kind).wait_send()
    for kind in (2, 3):
        gather(kind).wait_recv()
    keep_rest.wait()
    for which in (0, 1):
        for p in range(pieces):
            grad_out(which, p).wait()


def fused_scratch(n, m, seqs, tokens, width, inner, half, step):
    pieces = inner // half
    part = tokens // m
    cap = min(n * tokens, seqs * MAX_LEN)
    chunks = width // step
    dma = pltpu.SemaphoreType.DMA
    vmem = pltpu.VMEM
    bf16, f32 = jnp.bfloat16, jnp.float32
    buffers = [
        vmem((1, width), f32), vmem((n, seqs), jnp.int32), vmem((n, seqs), jnp.int32),
        vmem((n, seqs), jnp.int32), vmem((part, width), bf16),
        vmem((tokens, width), bf16), vmem((n, tokens, width), bf16),
        vmem((2, pieces, width, half), bf16),
        vmem((pieces, n, tokens, 2 * half), bf16), vmem((pieces, n, tokens, 2 * half), bf16),
        vmem((n, tokens, inner), bf16), vmem((n, tokens, inner), bf16),
        vmem((n, tokens, LANES), f32), vmem((n, tokens), f32),
        vmem((n, cap, n * tokens), bf16), vmem((n, 16, cap), f32), vmem((cap, 2 * half), bf16),
        vmem((tokens, width), f32), vmem((tokens, width), bf16), vmem((m, part, width), bf16),
    ]
    pair = lambda *shape: [dma(shape), dma(shape)]
    sems = [pltpu.SemaphoreType.REGULAR, dma((6,)), dma((2, pieces)), dma((3,)), dma((2, pieces))]
    sems += pair(2, n - 1, pieces) + [dma((n,)), dma((n, pieces, 4))]
    sems += pair(2, n - 1, pieces) + [dma(()), dma((pieces,))]
    sems += pair(2, n) + [dma((2, n)), dma((2, n, 4))] + [dma(()), dma((m,))] + pair(4)
    return buffers, sems


def fused_fits(n, m, seqs, tokens, width, inner):
    if m != 4 or n < 2 or tokens != LANES or inner < 4 * LANES or n * seqs > 256:
        return False
    buffers, _ = fused_scratch(n, m, seqs, tokens, width, inner, 2 * LANES, 4 * LANES)
    size = 0
    for buffer in buffers:
        count = jnp.dtype(buffer.dtype).itemsize
        for extent in buffer.shape:
            count *= extent
        size += count
    return size + tokens * width * 2 < 48 * 2**20


def fused(n, m, states, gains, proj_a, proj_b, cotangent, src_len, tgt_len, dest):
    _, tokens, width = states.shape
    inner = proj_a.shape[2]
    buffers, sems = fused_scratch(n, m, src_len.shape[1], tokens, width, inner, 2 * LANES, 4 * LANES)
    bf16 = jnp.bfloat16
    grad = jax.ShapeDtypeStruct((n, tokens, inner), bf16)
    slices = jax.ShapeDtypeStruct((n, tokens, width // n), bf16)
    hbm = pl.BlockSpec(memory_space=pltpu.HBM)
    return pl.pallas_call(
        functools.partial(fused_kernel, n, m),
        out_shape=(jax.ShapeDtypeStruct((tokens, width), bf16), grad, grad, slices, slices),
        in_specs=[hbm] * 8,
        out_specs=[hbm] * 5,
        scratch_shapes=buffers + sems,
        compiler_params=pltpu.CompilerParams(
            collective_id=2, has_side_effects=True, vmem_limit_bytes=56 * 2**20
        ),
        name="fused",
    )(states, cotangent, gains, src_len, tgt_len, dest, proj_a, proj_b)


def grads_kernel(
    left_a, left_b, right_a, right_b, states_in, out_a, out_b, states_out,
    left, right, states, out, left_sem, right_sem, states_sem, out_sem,
):
    tiles, tile = out.shape[1:3]
    loads = []
    for which, (src_left, src_right) in enumerate(((left_a, right_a), (left_b, right_b))):
        loads.append((
            pltpu.make_async_copy(src_right, right.at[which], right_sem.at[which]),
            pltpu.make_async_copy(src_left, left.at[which], left_sem.at[which]),
        ))
    for pair in loads:
        for copy in pair:
            copy.start()
    bring = pltpu.make_async_copy(states_in, states, states_sem.at[0])
    give = pltpu.make_async_copy(states, states_out.at[0], states_sem.at[1])
    bring.start()

    def store(which, t):
        at = pl.ds(pl.multiple_of(t * tile, tile), tile)
        return pltpu.make_async_copy(
            out.at[which, t], (out_a, out_b)[which].at[0, at, :], out_sem.at[which, t]
        )

    for which in (0, 1):
        for copy in loads[which]:
            copy.wait()
        for t in range(tiles):
            part = left[which, :, t * tile : (t + 1) * tile]
            out[which, t] = left_product(part, right[which])
            store(which, t).start()
        if which == 0:
            bring.wait()
            give.start()
    for which in (0, 1):
        for t in range(tiles):
            store(which, t).wait()
    give.wait()


def grads(left_a, left_b, right_a, right_b, states):
    rows, cols = left_a.shape
    inner = right_a.shape[1]
    tokens, width = states.shape
    tile = min(cols, 2 * LANES)
    tiles = cols // tile
    bf16, f32 = jnp.bfloat16, jnp.float32
    dma = pltpu.SemaphoreType.DMA
    hbm = pl.BlockSpec(memory_space=pltpu.HBM)
    return pl.pallas_call(
        grads_kernel,
        out_shape=(
            jax.ShapeDtypeStruct((1, cols, inner), f32),
            jax.ShapeDtypeStruct((1, cols, inner), f32),
            jax.ShapeDtypeStruct((1, tokens, width), bf16),
        ),
        in_specs=[hbm] * 5,
        out_specs=[hbm] * 3,
        scratch_shapes=[
            pltpu.VMEM((2, rows, cols), bf16), pltpu.VMEM((2, rows, inner), bf16),
            pltpu.VMEM((tokens, width), bf16), pltpu.VMEM((2, tiles, tile, inner), f32),
            dma((2,)), dma((2,)), dma((2,)), dma((2, tiles)),
        ],
        compiler_params=pltpu.CompilerParams(vmem_limit_bytes=62 * 2**20),
        name="grads",
    )(left_a, left_b, right_a, right_b, states)


def per_device(states, gains, proj_a, proj_b, cotangent, src_len, tgt_len, dest):
    n = lax.axis_size("dp")
    m = lax.axis_size("mp")
    _, tokens, width = states.shape
    inner = proj_a.shape[2]
    args = (states, gains, proj_a, proj_b, cotangent, src_len, tgt_len, dest)
    if not fused_fits(n, m, src_len.shape[1], tokens, width, inner):
        return stepwise(*args)
    result, grad_first, grad_second, mine_a, mine_b = fused(n, m, *args)
    rows = n * tokens
    grad_a, grad_b, grad_states = grads(
        mine_a.reshape(rows, -1), mine_b.reshape(rows, -1),
        grad_first.reshape(rows, -1), grad_second.reshape(rows, -1), result,
    )
    return (grad_states, grad_a, grad_b)


def solution(mesh):
    return jax.shard_map(
        per_device,
        mesh=mesh,
        in_specs=(
            P("section", "dp", None),
            P("section", None),
            P("section", None, "mp"),
            P("section", None, "mp"),
            P("dp", None),
            P(),
            P(),
            P(),
        ),
        out_specs=(P("section", "dp", None), P("section", "dp", "mp"), P("section", "dp", "mp")),
        check_vma=False,
    )
```
